512 devices in a mesh: rows: 128 (over y, z, core), grp: 4 (over x).
Axes of the slice: x: 4, y: 8, z: 8, core: 2. Of those that a mesh axis runs over, the one named last changes fastest.
Arguments:
- tiles: float32 [24576, 128, 128], P(('rows', 'grp')), may hold values from 0 to 24
- coords: int32 [24576, 2], P(('rows', 'grp')), may hold values from 0 to 2047, as said below
- live: int32 [512], P(('rows', 'grp')), may hold values from 6 to 48, as said below
- sketch: float32 [262144, 64], P(('rows', 'grp')), may hold values from -6 to 6
Outputs:
- basis: float32 [262144, 64], P(('rows', 'grp'))
The draws below stay inside these ranges and needn't reach their ends.
Inputs may be any that keep to these rules, and one draw needn't show every extreme that they name: `coords`: slot s of device d (slot d * 48 + s) has the row tile d * 4 + s and the column tile equal to it for s < 4; every other slot of device d has a row tile from d * 4 to d * 4 + 3, and a column tile in row block b - 1, b or b + 1 (modulo 128), where b = d // 4 and row block b is the tiles b * 16 to b * 16 + 15; slot 4 has its column tile in row block b - 1 and slot 5 in row block b + 1. The same coordinate pair may repeat. `live`: every device uses its slots 4 and 5; some device uses all 48.
All inputs are finite; a program needn't handle non-finite values.
Results may differ from the reference program's by a relative error of at most 0.0003.
Values sent between devices are 32-bit elements; how exact they have to be, the bound alone decides.
No kernel may reach another device: no remote copies, remote signals or barrier semaphores. Data moves between devices by JAX's collectives and lax.ppermute only.
A program may use at most 64 MiB of HBM per device.

```python
import math
import jax
import jax.numpy as jnp
from jax import lax

TILE = 128
K = 64
TPD = 4
CAP = 48
NROWS = 262144
N_ROWS = 128
N_GRP = 4
DEVICES = 512


def slot_layout(key):
    slot_ids = jnp.arange(DEVICES * CAP, dtype=jnp.int32)
    device = slot_ids // CAP
    within = slot_ids % CAP
    own_row = device * TPD + jax.random.randint(jax.random.fold_in(key, 21), (DEVICES * CAP,), 0, TPD)
    row_tile = jnp.where(within < TPD, device * TPD + within, own_row)
    step_off = jax.random.randint(jax.random.fold_in(key, 22), (DEVICES * CAP,), -1, 2)
    step_off = jnp.where(within == TPD, -1, jnp.where(within == TPD + 1, 1, step_off))
    col_block = (device // N_GRP + step_off + N_ROWS) % N_ROWS
    col_pick = jax.random.randint(jax.random.fold_in(key, 23), (DEVICES * CAP,), 0, N_GRP * TPD)
    col_tile = jnp.where(within < TPD, row_tile, col_block * N_GRP * TPD + col_pick)
    return jnp.stack([row_tile, col_tile], axis=1).astype(jnp.int32)


def slot_counts(key):
    levels = jax.random.randint(jax.random.fold_in(key, 31), (DEVICES,), 0, 16)
    counts = TPD + 2 + (CAP - TPD - 2) * levels * levels * levels // 4096
    fullest = jax.random.randint(jax.random.fold_in(key, 32), (), 0, DEVICES)
    return jnp.where(jnp.arange(DEVICES, dtype=jnp.int32) == fullest, CAP, counts).astype(jnp.int32)


def hub_profile(key):
    ratio_top = 6.0
    lift = 0.86 * ratio_top ** 0.25 * (2.0 * math.log(ratio_top) * NROWS / K) ** 0.125
    ordering = jax.random.permutation(jax.random.fold_in(key, 53), NROWS).astype(jnp.float32)
    falling = jnp.exp(-ordering * (math.log(ratio_top) / (4.0 * K)))
    return jnp.minimum(lift * falling, 4.5)


def node_weights(key):
    ramp = jnp.arange(NROWS, dtype=jnp.float32) / NROWS
    hubs = hub_profile(key)
    rough = jax.random.uniform(jax.random.fold_in(key, 52), (NROWS,), jnp.float32, -0.15, 0.15)
    jitter = jax.random.uniform(jax.random.fold_in(key, 54), (NROWS,), jnp.float32, -0.05, 0.05)
    return jnp.maximum(jnp.exp(-0.4 + 0.4 * ramp + rough), hubs * jnp.exp(jitter))


def draw_coords(key, part):
    return slot_layout(key)


def draw_live(key, part):
    return slot_counts(key)


def draw_tiles(key, part):
    shape = (DEVICES * CAP, TILE, TILE)
    spots = slot_layout(key)
    weights = node_weights(key).reshape(DEVICES * TPD, TILE)
    row_weight = weights[spots[:, 0]]
    col_weight = weights[spots[:, 1]]
    noise = jax.random.uniform(jax.random.fold_in(key, 41), shape, jnp.float32, 0.0, 1.0)
    within = jnp.arange(DEVICES * CAP, dtype=jnp.int32) % CAP
    diagonal = (within < TPD)[:, None, None]
    eye_tile = jnp.eye(TILE, dtype=jnp.float32)[None, :, :]
    near = 0.6 * eye_tile + noise * (1.0 / TILE)
    far = noise * (0.6 / TILE)
    affinity = jnp.where(diagonal, near, far)
    return (row_weight[:, :, None] * affinity * col_weight[:, None, :]).astype(jnp.float32)


def level_of(rng, extent, split, least, high):
    level = 1.0
    for axis_at, blocks in split:
        draws = jax.random.uniform(jax.random.fold_in(jax.random.fold_in(rng, 6), axis_at), (blocks,), jnp.float32, least / len(split), high / len(split))
        level = level * jnp.repeat(jnp.exp(draws), extent[axis_at] // blocks).reshape((-1,) + (1,) * (len(extent) - 1 - axis_at))
    return level


def gaussian(key, extent, deviation, reach, shards=(), held_as=jnp.bfloat16):
    factor_of = level_of(key, extent, shards, -0.22, 0.18) if shards else 1.0
    entries = jax.random.normal(key, extent, jnp.float32) * deviation * factor_of
    return jnp.minimum(jnp.maximum(entries, -reach), reach).astype(held_as)


def setup_inputs(seed: int = 0) -> dict:
    splits = jax.random.split(jax.random.key(seed), 5)
    return {
        "tiles": draw_tiles(jax.random.fold_in(splits[4], 71), 0),
        "coords": draw_coords(jax.random.fold_in(splits[4], 71), 0),
        "live": draw_live(jax.random.fold_in(splits[4], 71), 0),
        "sketch": gaussian(splits[3], (NROWS, K), 1.0, 6.0, ((0, 512),), jnp.float32),
    }


HIGHEST = lax.Precision.HIGHEST

def apply_graph(tiles, coords, live, panel, transpose):
    panel_tiles = panel.reshape(DEVICES * TPD, TILE, K)
    initial = jnp.zeros((DEVICES * TPD, TILE, K), jnp.float32)
    slot_ids = jnp.arange(CAP, dtype=jnp.int32)

    def device_step(device, summed):
        offset = (device * CAP).astype(jnp.int32)
        tile_slab = lax.dynamic_slice_in_dim(tiles, offset, CAP, 0)
        spots = lax.dynamic_slice_in_dim(coords, offset, CAP, 0)
        active = (slot_ids < live[device]).astype(jnp.float32)
        if transpose:
            fetched = panel_tiles[spots[:, 0]]
            product = jnp.einsum('sji,sjk->sik', tile_slab, fetched, precision=HIGHEST)
            placed = spots[:, 1]
        else:
            fetched = panel_tiles[spots[:, 1]]
            product = jnp.einsum('sij,sjk->sik', tile_slab, fetched, precision=HIGHEST)
            placed = spots[:, 0]
        return summed.at[placed].add(product * active[:, None, None])
    result = lax.fori_loop(0, DEVICES, device_step, initial)
    return result.reshape(DEVICES * TPD * TILE, K)

def orthonormal(image):
    gram = jnp.dot(image.T.astype(jnp.float32), image.astype(jnp.float32), precision=HIGHEST, preferred_element_type=jnp.float32)
    lower = jnp.linalg.cholesky(gram)
    return jax.scipy.linalg.solve_triangular(lower, image.T, lower=True).T

def reference(tiles, coords, live, sketch):
    panel = sketch
    for sweep in range(2):
        spread = apply_graph(tiles, coords, live, panel, True)
        image = apply_graph(tiles, coords, live, spread, False)
        panel = orthonormal(image)
    return panel * NROWS ** 0.5
```

```python
import functools

import jax
import jax.numpy as jnp
from jax import lax
from jax.experimental import pallas as pl
from jax.experimental.pallas import tpu as pltpu
from jax.sharding import Mesh
from jax.sharding import PartitionSpec as P

ROWS = ("y", "z", "c")
ROWS_GRP = ("y", "z", "c", "grp")
HIGHEST = lax.Precision.HIGHEST
F32 = jnp.float32
BF16 = jnp.bfloat16
T = 128
CHUNK = 8


def dot(a, b, contract, precision=None):
    return lax.dot_general(
        a, b, ((contract[:1], contract[1:]), ((), ())), precision=precision, preferred_element_type=F32
    )


def halves(x):
    hi = x.astype(BF16)
    return hi, (x - hi.astype(F32)).astype(BF16)


def fold(q, k):
    return (q[:k, :T] + q[k:, T:]) + (q[k:, :T] + q[:k, T:])


def start_tiles(live, tiles, tbuf, sems, cap):
    for c in range(cap // CHUNK):
        at = pl.ds(c * CHUNK, CHUNK)

        @pl.when(c * CHUNK < live)
        def _():
            pltpu.make_async_copy(tiles.at[at], tbuf.at[at], sems.at[c]).start()


def each_chunk(live, tiles, tbuf, sems, cap, work, wait=True):
    for c in range(cap // CHUNK):
        at = pl.ds(c * CHUNK, CHUNK)

        @pl.when(c * CHUNK < live)
        def _():
            if wait:
                pltpu.make_async_copy(tiles.at[at], tbuf.at[at], sems.at[c]).wait()
            for s in range(c * CHUNK, (c + 1) * CHUNK):
                work(s)


def keep_panel(panel, k, phl):
    for t in range(phl.shape[0]):
        hi, lo = halves(panel(t))
        phl[t, :k, :] = hi
        phl[t, k:, :] = lo


def spread_slot(s, code, hi, lo, phl, acc):
    k = phl.shape[1] // 2
    entry = code[s]
    at = entry & 255
    q = dot(phl[entry >> 8], jnp.concatenate([hi, lo], axis=1), (1, 0))
    acc[at] += fold(q, k)


def put_spread(acc, outs):
    each = outs[0].shape[0]
    for n, out in enumerate(outs):
        out[...] = acc[n * each : (n + 1) * each]


def first_kernel(code, live, tiles, sketch, outer, own, partner, tbuf, phl, acc, sems):
    cap = tiles.shape[0]
    k = sketch.shape[1]
    start_tiles(live[0], tiles, tbuf, sems, cap)
    acc[...] = jnp.zeros_like(acc)
    keep_panel(lambda t: sketch[t * T : (t + 1) * T, :].T, k, phl)

    def work(s):
        hi, lo = halves(tbuf[s])
        spread_slot(s, code, hi, lo, phl, acc)

    each_chunk(live[0], tiles, tbuf, sems, cap, work)
    put_spread(acc, (outer, own, partner))


def keep_spread(parts, shl):
    k = parts[0].shape[1]
    each = parts[0].shape[0]
    for n, part in enumerate(parts):

        def one(i, carry, part=part, n=n):
            hi, lo = halves(part[i])
            shl[n * each + i, :k, :] = hi
            shl[n * each + i, k:, :] = lo
            return carry

        lax.fori_loop(0, each, one, 0, unroll=4)
    shl[3 * each] = jnp.zeros_like(shl[3 * each])


def image_slot(s, code, hi, lo, shl, img):
    k = shl.shape[1] // 2
    entry = code[s]
    q = dot(shl[entry & 255], jnp.concatenate([hi, lo], axis=0), (1, 1))
    img[entry >> 8] += fold(q, k)


def whole_image(img):
    return jnp.concatenate([img[t] for t in range(img.shape[0])], axis=1)


def put_gram(image, out):
    g = dot(image, image, (1, 1), HIGHEST)
    half = g.shape[0] // 2
    out[...] = jnp.concatenate([g[:half], g[half:]], axis=1)


def middle_kernel(
    code, live, tiles, s_outer, s_own, s_partner, outer, own, partner, gram,
    tbuf, thl, shl, img, phl, acc, sems,
):
    cap = tiles.shape[0]
    k = s_own.shape[1]
    start_tiles(live[0], tiles, tbuf, sems, cap)
    keep_spread((s_outer, s_own, s_partner), shl)
    img[...] = jnp.zeros_like(img)
    acc[...] = jnp.zeros_like(acc)

    def forth(s):
        hi, lo = halves(tbuf[s])
        thl[s, :T, :] = hi
        thl[s, T:, :] = lo
        image_slot(s, code, hi, lo, shl, img)

    each_chunk(live[0], tiles, tbuf, sems, cap, forth)
    put_gram(whole_image(img), gram)
    keep_panel(lambda t: img[t], k, phl)

    def back(s):
        spread_slot(s, code, thl[s, :T, :], thl[s, T:, :], phl, acc)

    each_chunk(live[0], tiles, tbuf, sems, cap, back, wait=False)
    put_spread(acc, (outer, own, partner))


def inverse_factor(g):
    k = g.shape[0]
    row_id = lax.broadcasted_iota(jnp.int32, (8, 2 * k), 0)
    eye = (lax.broadcasted_iota(jnp.int32, (k, k), 0) == lax.broadcasted_iota(jnp.int32, (k, k), 1)).astype(F32)
    full = jnp.concatenate([g, eye], axis=1)
    m = [full[8 * j : 8 * j + 8] for j in range(k // 8)]

    def row_of(x, r):
        return jnp.broadcast_to(x[r : r + 1, :], x.shape)

    for j in range(k // 8):
        rows = [row_of(m[j], t) for t in range(8)]
        cols = [
            {i: jnp.broadcast_to(m[i][:, 8 * j + t : 8 * j + t + 1], (8, 2 * k)) for i in range(j, k // 8)}
            for t in range(8)
        ]
        scale = jnp.zeros((8, 2 * k), F32)
        for t in range(8):
            pivot = row_of(cols[t][j], t)
            scale = jnp.where(row_id == t, lax.rsqrt(pivot), scale)
            inv = 1.0 / pivot
            q = rows[t] * inv
            cols[t][j] = jnp.where(row_id > t, cols[t][j], 0.0)
            for u in range(t + 1, 8):
                part = row_of(cols[t][j], u)
                f = part * inv
                rows[u] = rows[u] - part * q
                for i in range(j, k // 8):
                    cols[u][i] = cols[u][i] - cols[t][i] * f
            for i in range(j, k // 8):
                m[i] = m[i] - cols[t][i] * q
        m[j] = m[j] * scale
    return jnp.concatenate([x[:, k:] for x in m], axis=0)


def summed_gram(parts):
    g = parts[0]
    for n in range(1, parts.shape[0]):
        g = g + parts[n]
    half = g.shape[1] // 2
    return jnp.concatenate([g[:, :half], g[:, half:]], axis=0)


def factor_kernel(parts, linv):
    linv[...] = inverse_factor(summed_gram(parts))


def last_kernel(code, live, tiles, s_outer, s_own, s_partner, linv, image, gram, tbuf, shl, img, sems):
    cap = tiles.shape[0]
    start_tiles(live[0], tiles, tbuf, sems, cap)
    keep_spread((s_outer, s_own, s_partner), shl)
    img[...] = jnp.zeros_like(img)

    def forth(s):
        hi, lo = halves(tbuf[s])
        image_slot(s, code, hi, lo, shl, img)

    each_chunk(live[0], tiles, tbuf, sems, cap, forth)
    x = dot(linv[...], whole_image(img), (1, 0), HIGHEST)
    image[...] = x
    put_gram(x, gram)


def basis_kernel(parts, image, basis, *, scale):
    linv = inverse_factor(summed_gram(parts))
    basis[...] = dot(linv, image[...], (1, 0), HIGHEST).T * scale


def to_everyone(x, axes):
    peers = lax.axis_size(axes)
    copies = jnp.broadcast_to(x, (peers, *x.shape))
    return lax.all_to_all(copies, axes, split_axis=0, concat_axis=0, tiled=True)


VMEM = pl.BlockSpec(memory_space=pltpu.VMEM)
ANY = pl.BlockSpec(memory_space=pl.ANY)


def local(tiles, coords, live, sketch):
    rows = lax.axis_size(ROWS)
    groups = lax.axis_size("grp")
    cap = tiles.shape[0]
    k = sketch.shape[1]
    mine = sketch.shape[0] // T
    block = groups * mine
    row = lax.axis_index(ROWS)
    odd = lax.axis_index("c")

    step = (coords[:, 1] // block - row + 1 + rows) % rows
    step = jnp.where(odd == 1, 2 - step, step)
    place = step * block + coords[:, 1] % block
    place = jnp.where(jnp.arange(cap, dtype=jnp.int32) < live[0], place, 3 * block)
    code = place + 256 * (coords[:, 0] % mine)

    outer = [(r, (r - 1) % rows if r % 2 == 0 else (r + 1) % rows) for r in range(rows)]
    partner = [(r, r ^ 1) for r in range(rows)]

    block_shape = jax.ShapeDtypeStruct((block, k, T), F32)
    gram_shape = jax.ShapeDtypeStruct((k // 2, 2 * k), F32)
    square = jax.ShapeDtypeStruct((k, k), F32)
    tbuf = pltpu.VMEM((cap, T, T), F32)
    thl = pltpu.VMEM((cap, 2 * T, T), BF16)
    phl = pltpu.VMEM((mine, 2 * k, T), BF16)
    shl = pltpu.VMEM((3 * block + 1, 2 * k, T), BF16)
    acc = pltpu.VMEM((3 * block + 1, k, T), F32)
    img = pltpu.VMEM((mine, k, T), F32)
    sems = pltpu.SemaphoreType.DMA((cap // CHUNK,))

    def call(kernel, ins, outs, scratch, prefetch=0, name=None):
        return pl.pallas_call(
            kernel,
            grid_spec=pltpu.PrefetchScalarGridSpec(
                num_scalar_prefetch=prefetch, grid=(), in_specs=ins, out_specs=[VMEM] * len(outs), scratch_shapes=scratch
            ),
            out_shape=outs,
            name=name,
            compiler_params=pltpu.CompilerParams(vmem_limit_bytes=48 * 1024 * 1024),
        )

    def exchange(parts, extra=None):
        p_outer, p_own, p_partner = parts
        got_outer = lax.ppermute(p_outer, ROWS, outer)
        got_partner = lax.ppermute(p_partner, ROWS, partner)
        total = p_own + got_outer + got_partner
        pieces = total.reshape(groups, mine, k, T)
        arrived = lax.all_to_all(pieces, "grp", split_axis=0, concat_axis=0, tiled=True)
        whole = to_everyone(arrived.sum(axis=0), "grp").reshape(block, k, T)
        return lax.ppermute(whole, ROWS, outer), whole, lax.ppermute(whole, ROWS, partner)

    def gram_parts(gram):
        gram = to_everyone(gram, ("c", "grp")).sum(axis=0)
        gram = to_everyone(gram, "z").sum(axis=0)
        return to_everyone(gram, "y")

    parts = call(first_kernel, [ANY, VMEM], [block_shape] * 3, [tbuf, phl, acc, sems], 2, "first")(
        code, live, tiles, sketch
    )
    whole = exchange(parts)
    *parts, gram = call(
        middle_kernel, [ANY] + [VMEM] * 3, [block_shape] * 3 + [gram_shape], [tbuf, thl, shl, img, phl, acc, sems], 2, "middle"
    )(code, live, tiles, *whole)
    linv = call(factor_kernel, [VMEM], [square], [], 0, "factor")(gram_parts(gram))[0]
    whole = exchange(parts)
    image, gram = call(
        last_kernel, [ANY] + [VMEM] * 4, [jax.ShapeDtypeStruct((k, mine * T), F32), gram_shape], [tbuf, shl, img, sems], 2, "last"
    )(code, live, tiles, *whole, linv)
    scale = float(rows * groups * sketch.shape[0]) ** 0.5
    return call(
        functools.partial(basis_kernel, scale=scale), [VMEM] * 2, [jax.ShapeDtypeStruct(sketch.shape, F32)], [], 0, "basis"
    )(gram_parts(gram), image)[0]


def solution(mesh):
    finer = Mesh(mesh.devices.reshape(8, 8, 2, mesh.shape["grp"]), ROWS_GRP)
    placed = (P(ROWS_GRP, None, None), P(ROWS_GRP, None), P(ROWS_GRP), P(ROWS_GRP, None))
    return jax.shard_map(local, mesh=finer, in_specs=placed, out_specs=P(ROWS_GRP, None), check_vma=False)
```

```python
import functools

import jax
import jax.numpy as jnp
from jax import lax
from jax.experimental import pallas as pl
from jax.experimental.pallas import tpu as pltpu
from jax.sharding import Mesh
from jax.sharding import PartitionSpec as P

ROWS = ("y", "z", "c")
ROWS_GRP = ("y", "z", "c", "grp")
HIGHEST = lax.Precision.HIGHEST
F32 = jnp.float32
BF16 = jnp.bfloat16
T = 128
CHUNK = 8


def dot(a, b, contract, precision=None):
    return lax.dot_general(
        a, b, ((contract[:1], contract[1:]), ((), ())), precision=precision, preferred_element_type=F32
    )


def halves(x):
    hi = x.astype(BF16)
    return hi, (x - hi.astype(F32)).astype(BF16)


def fold(q, k):
    return (q[:k, :T] + q[k:, T:]) + (q[k:, :T] + q[:k, T:])


def start_tiles(live, tiles, tbuf, sems, cap):
    for c in range(cap // CHUNK):
        at = pl.ds(c * CHUNK, CHUNK)

        @pl.when(c * CHUNK < live)
        def _():
            pltpu.make_async_copy(tiles.at[at], tbuf.at[at], sems.at[c]).start()


def each_chunk(live, tiles, tbuf, sems, cap, work, wait=True):
    for c in range(cap // CHUNK):
        at = pl.ds(c * CHUNK, CHUNK)

        @pl.when(c * CHUNK < live)
        def _():
            if wait:
                pltpu.make_async_copy(tiles.at[at], tbuf.at[at], sems.at[c]).wait()
            for s in range(c * CHUNK, (c + 1) * CHUNK):
                work(s)


def keep_panel(panel, k, phl):
    for t in range(phl.shape[0]):
        hi, lo = halves(panel(t))
        phl[t, :k, :] = hi
        phl[t, k:, :] = lo


def spread_slot(s, code, hi, lo, phl, acc):
    k = phl.shape[1] // 2
    entry = code[s]
    at = entry & 255
    q = dot(phl[entry >> 8], jnp.concatenate([hi, lo], axis=1), (1, 0))
    acc[at] += fold(q, k)


def put_spread(acc, outs):
    each = outs[0].shape[0]
    for n, out in enumerate(outs):
        out[...] = acc[n * each : (n + 1) * each]


def first_kernel(code, live, tiles, sketch, outer, own, partner, tbuf, phl, acc, sems):
    cap = tiles.shape[0]
    k = sketch.shape[0]
    start_tiles(live[0], tiles, tbuf, sems, cap)
    acc[...] = jnp.zeros_like(acc)
    keep_panel(lambda t: sketch[:, t * T : (t + 1) * T], k, phl)

    def work(s):
        hi, lo = halves(tbuf[s])
        spread_slot(s, code, hi, lo, phl, acc)

    each_chunk(live[0], tiles, tbuf, sems, cap, work)
    put_spread(acc, (outer, own, partner))


def keep_spread(parts, shl):
    k = parts[0].shape[1]
    each = parts[0].shape[0]
    for n, part in enumerate(parts):

        def one(i, carry, part=part, n=n):
            hi, lo = halves(part[i])
            shl[n * each + i, :k, :] = hi
            shl[n * each + i, k:, :] = lo
            return carry

        lax.fori_loop(0, each, one, 0, unroll=4)
    shl[3 * each] = jnp.zeros_like(shl[3 * each])


def image_slot(s, code, hi, lo, shl, img):
    k = shl.shape[1] // 2
    entry = code[s]
    q = dot(shl[entry & 255], jnp.concatenate([hi, lo], axis=0), (1, 1))
    img[entry >> 8] += fold(q, k)


def whole_image(img):
    return jnp.concatenate([img[t] for t in range(img.shape[0])], axis=1)


def put_gram(image, out):
    g = dot(image, image, (1, 1), HIGHEST)
    half = g.shape[0] // 2
    out[...] = jnp.concatenate([g[:half], g[half:]], axis=1)


def middle_kernel(
    code, live, tiles, s_outer, s_own, s_partner, outer, own, partner, gram,
    tbuf, thl, shl, img, phl, acc, sems,
):
    cap = tiles.shape[0]
    k = s_own.shape[1]
    start_tiles(live[0], tiles, tbuf, sems, cap)
    keep_spread((s_outer, s_own, s_partner), shl)
    img[...] = jnp.zeros_like(img)
    acc[...] = jnp.zeros_like(acc)

    def forth(s):
        hi, lo = halves(tbuf[s])
        thl[s, :T, :] = hi
        thl[s, T:, :] = lo
        image_slot(s, code, hi, lo, shl, img)

    each_chunk(live[0], tiles, tbuf, sems, cap, forth)
    put_gram(whole_image(img), gram)
    keep_panel(lambda t: img[t], k, phl)

    def back(s):
        spread_slot(s, code, thl[s, :T, :], thl[s, T:, :], phl, acc)

    each_chunk(live[0], tiles, tbuf, sems, cap, back, wait=False)
    put_spread(acc, (outer, own, partner))


def inverse_factor(g):
    k = g.shape[0]
    row_id = lax.broadcasted_iota(jnp.int32, (8, 2 * k), 0)
    eye = (lax.broadcasted_iota(jnp.int32, (k, k), 0) == lax.broadcasted_iota(jnp.int32, (k, k), 1)).astype(F32)
    full = jnp.concatenate([g, eye], axis=1)
    m = [full[8 * j : 8 * j + 8] for j in range(k // 8)]

    def row_of(x, r):
        return jnp.broadcast_to(x[r : r + 1, :], x.shape)

    for j in range(k // 8):
        rows = [row_of(m[j], t) for t in range(8)]
        cols = [
            {i: jnp.broadcast_to(m[i][:, 8 * j + t : 8 * j + t + 1], (8, 2 * k)) for i in range(j, k // 8)}
            for t in range(8)
        ]
        scale = jnp.zeros((8, 2 * k), F32)
        for t in range(8):
            pivot = row_of(cols[t][j], t)
            scale = jnp.where(row_id == t, lax.rsqrt(pivot), scale)
            inv = 1.0 / pivot
            q = rows[t] * inv
            cols[t][j] = jnp.where(row_id > t, cols[t][j], 0.0)
            for u in range(t + 1, 8):
                part = row_of(cols[t][j], u)
                f = part * inv
                rows[u] = rows[u] - part * q
                for i in range(j, k // 8):
                    cols[u][i] = cols[u][i] - cols[t][i] * f
            for i in range(j, k // 8):
                m[i] = m[i] - cols[t][i] * q
        m[j] = m[j] * scale
    return jnp.concatenate([x[:, k:] for x in m], axis=0)


def summed_gram(parts):
    g = parts[0]
    for n in range(1, parts.shape[0]):
        g = g + parts[n]
    half = g.shape[1] // 2
    return jnp.concatenate([g[:, :half], g[:, half:]], axis=0)


def factor_kernel(parts, linv):
    linv[...] = inverse_factor(summed_gram(parts))


def last_kernel(code, live, tiles, s_outer, s_own, s_partner, linv, image, gram, tbuf, shl, img, sems):
    cap = tiles.shape[0]
    start_tiles(live[0], tiles, tbuf, sems, cap)
    keep_spread((s_outer, s_own, s_partner), shl)
    img[...] = jnp.zeros_like(img)

    def forth(s):
        hi, lo = halves(tbuf[s])
        image_slot(s, code, hi, lo, shl, img)

    each_chunk(live[0], tiles, tbuf, sems, cap, forth)
    x = dot(linv[...], whole_image(img), (1, 0), HIGHEST)
    image[...] = x
    put_gram(x, gram)


def basis_kernel(parts, image, basis, *, scale):
    linv = inverse_factor(summed_gram(parts))
    basis[...] = dot(linv, image[...], (1, 0), HIGHEST) * scale


def to_everyone(x, axes):
    peers = lax.axis_size(axes)
    copies = jnp.broadcast_to(x, (peers, *x.shape))
    return lax.all_to_all(copies, axes, split_axis=0, concat_axis=0, tiled=True)


VMEM = pl.BlockSpec(memory_space=pltpu.VMEM)
ANY = pl.BlockSpec(memory_space=pl.ANY)


def local(tiles, coords, live, sketch):
    rows = lax.axis_size(ROWS)
    groups = lax.axis_size("grp")
    cap = tiles.shape[0]
    k = sketch.shape[1]
    mine = sketch.shape[0] // T
    block = groups * mine
    row = lax.axis_index(ROWS)
    odd = lax.axis_index("c")

    step = (coords[:, 1] // block - row + 1 + rows) % rows
    step = jnp.where(odd == 1, 2 - step, step)
    place = step * block + coords[:, 1] % block
    place = jnp.where(jnp.arange(cap, dtype=jnp.int32) < live[0], place, 3 * block)
    code = place + 256 * (coords[:, 0] % mine)

    outer = [(r, (r - 1) % rows if r % 2 == 0 else (r + 1) % rows) for r in range(rows)]
    partner = [(r, r ^ 1) for r in range(rows)]

    block_shape = jax.ShapeDtypeStruct((block, k, T), F32)
    gram_shape = jax.ShapeDtypeStruct((k // 2, 2 * k), F32)
    square = jax.ShapeDtypeStruct((k, k), F32)
    tbuf = pltpu.VMEM((cap, T, T), F32)
    thl = pltpu.VMEM((cap, 2 * T, T), BF16)
    phl = pltpu.VMEM((mine, 2 * k, T), BF16)
    shl = pltpu.VMEM((3 * block + 1, 2 * k, T), BF16)
    acc = pltpu.VMEM((3 * block + 1, k, T), F32)
    img = pltpu.VMEM((mine, k, T), F32)
    sems = pltpu.SemaphoreType.DMA((cap // CHUNK,))

    def call(kernel, ins, outs, scratch, prefetch=0, name=None):
        return pl.pallas_call(
            kernel,
            grid_spec=pltpu.PrefetchScalarGridSpec(
                num_scalar_prefetch=prefetch, grid=(), in_specs=ins, out_specs=[VMEM] * len(outs), scratch_shapes=scratch
            ),
            out_shape=outs,
            name=name,
            compiler_params=pltpu.CompilerParams(vmem_limit_bytes=48 * 1024 * 1024),
        )

    def over_grp(x):
        return lax.all_to_all(x, "grp", split_axis=0, concat_axis=0, tiled=True)

    def over_outer(x):
        return lax.ppermute(x, ROWS, outer)

    def over_partner(x):
        return lax.ppermute(x, ROWS, partner)

    def pieces(x):
        return x.reshape(groups, mine, k, T)

    def exchange(parts):
        p_outer, p_own, p_partner = parts
        got = over_partner(p_partner)
        at_outer = over_outer(over_grp(pieces(p_outer)).sum(axis=0))
        middle = over_grp(pieces(p_own + got)).sum(axis=0) + at_outer
        beside = over_outer(middle)
        own = to_everyone(middle, "grp").reshape(block, k, T)
        return to_everyone(beside, "grp").reshape(block, k, T), own, over_partner(own)

    def exchange_with_gram(parts, gram):
        p_outer, p_own, p_partner = parts
        got_outer = over_outer(p_outer)
        got = over_partner(p_partner)
        gram = to_everyone(gram, ("z", "c")).sum(axis=0)
        total = (p_own + got_outer + got).reshape(groups, mine * k, T)
        sides = jnp.broadcast_to(gram, (groups, *gram.shape))
        arrived = over_grp(jnp.concatenate([total, sides], axis=1)).sum(axis=0)
        middle, gram = arrived[: mine * k].reshape(mine, k, T), arrived[mine * k :]
        own = to_everyone(middle, "grp").reshape(block, k, T)
        own, gram = lax.optimization_barrier((own, gram))
        gram = to_everyone(gram, "y")
        return (over_outer(own), own, over_partner(own)), gram

    def gram_parts(gram):
        gram = to_everyone(gram, ("c", "grp")).sum(axis=0)
        gram = to_everyone(gram, "z").sum(axis=0)
        return to_everyone(gram, "y")

    parts = call(first_kernel, [ANY, VMEM], [block_shape] * 3, [tbuf, phl, acc, sems], 2, "first")(
        code, live, tiles, sketch.T
    )
    whole = exchange(parts)
    *parts, gram = call(
        middle_kernel, [ANY] + [VMEM] * 3, [block_shape] * 3 + [gram_shape], [tbuf, thl, shl, img, phl, acc, sems], 2, "middle"
    )(code, live, tiles, *whole)
    whole, gram = exchange_with_gram(parts, gram)
    linv = call(factor_kernel, [VMEM], [square], [], 0, "factor")(gram)[0]
    image, gram = call(
        last_kernel, [ANY] + [VMEM] * 4, [jax.ShapeDtypeStruct((k, mine * T), F32), gram_shape], [tbuf, shl, img, sems], 2, "last"
    )(code, live, tiles, *whole, linv)
    scale = float(rows * groups * sketch.shape[0]) ** 0.5
    return call(
        functools.partial(basis_kernel, scale=scale), [VMEM] * 2, [jax.ShapeDtypeStruct(sketch.shape[::-1], F32)], [], 0, "basis"
    )(gram_parts(gram), image)[0].T


def solution(mesh):
    finer = Mesh(mesh.devices.reshape(8, 8, 2, mesh.shape["grp"]), ROWS_GRP)
    placed = (P(ROWS_GRP, None, None), P(ROWS_GRP, None), P(ROWS_GRP), P(ROWS_GRP, None))
    return jax.shard_map(local, mesh=finer, in_specs=placed, out_specs=P(ROWS_GRP, None), check_vma=False)
```

```python
import functools

import jax
import jax.numpy as jnp
from jax import lax
from jax.experimental import pallas as pl
from jax.experimental.pallas import tpu as pltpu
from jax.sharding import Mesh
from jax.sharding import PartitionSpec as P


ROWS = ("y", "z", "c")
ROWS_GRP = ("y", "z", "c", "grp")
HIGHEST = lax.Precision.HIGHEST
F32 = jnp.float32
BF16 = jnp.bfloat16
T = 128
CHUNK = 8
VMEM_LIMIT = 48 * 1024 * 1024


def dot(a, b, contract, precision=None):
    return lax.dot_general(
        a, b, ((contract[:1], contract[1:]), ((), ())), precision=precision, preferred_element_type=F32
    )


def halves(x):
    hi = x.astype(BF16)
    return hi, (x - hi.astype(F32)).astype(BF16)


def fold(q, k):
    return (q[:k, :T] + q[k:, T:]) + (q[k:, :T] + q[:k, T:])


def each_chunk(live, cap, work, ready=None):
    for c in range(cap // CHUNK):

        @pl.when(c * CHUNK < live)
        def _():
            if ready is not None:
                ready(c)
            for s in range(c * CHUNK, (c + 1) * CHUNK):
                work(s)


def keep_panel(panel, k, phl):
    for t in range(phl.shape[0]):
        hi, lo = halves(panel(t))
        phl[t, :k, :] = hi
        phl[t, k:, :] = lo


def spread_slot(s, code, thl, phl, acc):
    k = phl.shape[1] // 2
    entry = code[s]
    at = entry & 255
    q = dot(phl[entry >> 8], jnp.concatenate([thl[s, :T, :], thl[s, T:, :]], axis=1), (1, 0))
    acc[at] += fold(q, k)


def put_spread(acc, outs):
    each = outs[0].shape[0]
    for n, out in enumerate(outs):
        out[...] = acc[n * each : (n + 1) * each]


def first_kernel(
    code, live, tiles, sketch, outer, own, partner, thl, tbuf, panel, phl, acc, sems, panel_sem
):
    cap = tiles.shape[0]
    k = sketch.shape[0]

    def tile_copy(c):
        at = pl.ds(c * CHUNK, CHUNK)
        return pltpu.make_async_copy(tiles.at[at], tbuf.at[at], sems.at[c])

    panel_copy = pltpu.make_async_copy(sketch, panel, panel_sem)
    panel_copy.start()
    for c in range(cap // CHUNK):

        @pl.when(c * CHUNK < live[0])
        def _():
            tile_copy(c).start()

    acc[...] = jnp.zeros_like(acc)
    panel_copy.wait()
    keep_panel(lambda t: panel[:, t * T : (t + 1) * T], k, phl)

    def work(s):
        hi, lo = halves(tbuf[s])
        thl[s, :T, :] = hi
        thl[s, T:, :] = lo
        spread_slot(s, code, thl, phl, acc)

    each_chunk(live[0], cap, work, lambda c: tile_copy(c).wait())
    put_spread(acc, (outer, own, partner))


def keep_spread(parts, shl):
    k = parts[0].shape[1]
    each = parts[0].shape[0]
    for n, part in enumerate(parts):

        def one(i, carry, part=part, n=n):
            hi, lo = halves(part[i])
            shl[n * each + i, :k, :] = hi
            shl[n * each + i, k:, :] = lo
            return carry

        lax.fori_loop(0, each, one, 0, unroll=4)
    shl[3 * each] = jnp.zeros_like(shl[3 * each])


def image_slot(s, code, thl, shl, img):
    k = shl.shape[1] // 2
    entry = code[s]
    q = dot(shl[entry & 255], thl[s], (1, 1))
    img[entry >> 8] += fold(q, k)


def whole_image(img):
    return jnp.concatenate([img[t] for t in range(img.shape[0])], axis=1)


def put_gram(image, out):
    g = dot(image, image, (1, 1), HIGHEST)
    half = g.shape[0] // 2
    out[...] = jnp.concatenate([g[:half], g[half:]], axis=1)


def middle_kernel(
    code, live, thl, s_outer, s_own, s_partner, outer, own, partner, gram, shl, img, phl, acc
):
    cap = thl.shape[0]
    k = s_own.shape[1]
    keep_spread((s_outer, s_own, s_partner), shl)
    img[...] = jnp.zeros_like(img)
    acc[...] = jnp.zeros_like(acc)
    each_chunk(live[0], cap, lambda s: image_slot(s, code, thl, shl, img))
    put_gram(whole_image(img), gram)
    keep_panel(lambda t: img[t], k, phl)
    each_chunk(live[0], cap, lambda s: spread_slot(s, code, thl, phl, acc))
    put_spread(acc, (outer, own, partner))


def inverse_factor(g):
    k = g.shape[0]
    row_id = lax.broadcasted_iota(jnp.int32, (8, 2 * k), 0)
    eye = (lax.broadcasted_iota(jnp.int32, (k, k), 0) == lax.broadcasted_iota(jnp.int32, (k, k), 1)).astype(F32)
    full = jnp.concatenate([g, eye], axis=1)
    m = [full[8 * j : 8 * j + 8] for j in range(k // 8)]

    def row_of(x, r):
        return jnp.broadcast_to(x[r : r + 1, :], x.shape)

    for j in range(k // 8):
        rows = [row_of(m[j], t) for t in range(8)]
        cols = [
            {i: jnp.broadcast_to(m[i][:, 8 * j + t : 8 * j + t + 1], (8, 2 * k)) for i in range(j, k // 8)}
            for t in range(8)
        ]
        scale = jnp.zeros((8, 2 * k), F32)
        for t in range(8):
            pivot = row_of(cols[t][j], t)
            scale = jnp.where(row_id == t, lax.rsqrt(pivot), scale)
            inv = 1.0 / pivot
            q = rows[t] * inv
            cols[t][j] = jnp.where(row_id > t, cols[t][j], 0.0)
            for u in range(t + 1, 8):
                part = row_of(cols[t][j], u)
                f = part * inv
                rows[u] = rows[u] - part * q
                for i in range(j, k // 8):
                    cols[u][i] = cols[u][i] - cols[t][i] * f
            for i in range(j, k // 8):
                m[i] = m[i] - cols[t][i] * q
        m[j] = m[j] * scale
    return jnp.concatenate([x[:, k:] for x in m], axis=0)


def summed_gram(parts):
    g = parts[0]
    for n in range(1, parts.shape[0]):
        g = g + parts[n]
    half = g.shape[1] // 2
    return jnp.concatenate([g[:, :half], g[:, half:]], axis=0)


def factor_kernel(parts, linv):
    linv[...] = inverse_factor(summed_gram(parts))


def last_kernel(code, live, thl, s_outer, s_own, s_partner, linv, image, gram, shl, img):
    keep_spread((s_outer, s_own, s_partner), shl)
    img[...] = jnp.zeros_like(img)
    each_chunk(live[0], thl.shape[0], lambda s: image_slot(s, code, thl, shl, img))
    x = dot(linv[...], whole_image(img), (1, 0), HIGHEST)
    image[...] = x
    put_gram(x, gram)


def basis_kernel(parts, image, basis, *, scale):
    linv = inverse_factor(summed_gram(parts))
    basis[...] = dot(linv, image[...], (1, 0), HIGHEST) * scale


def to_everyone(x, axes):
    peers = lax.axis_size(axes)
    copies = jnp.broadcast_to(x, (peers, *x.shape))
    return lax.all_to_all(copies, axes, split_axis=0, concat_axis=0, tiled=True)


VMEM = pl.BlockSpec(memory_space=pltpu.VMEM)
HBM = pl.BlockSpec(memory_space=pltpu.HBM)


def local(tiles, coords, live, sketch):
    rows = lax.axis_size(ROWS)
    groups = lax.axis_size("grp")
    cap = tiles.shape[0]
    k = sketch.shape[1]
    mine = sketch.shape[0] // T
    block = groups * mine
    row = lax.axis_index(ROWS)
    odd = lax.axis_index("c")

    step = (coords[:, 1] // block - row + 1 + rows) % rows
    step = jnp.where(odd == 1, 2 - step, step)
    place = step * block + coords[:, 1] % block
    place = jnp.where(jnp.arange(cap, dtype=jnp.int32) < live[0], place, 3 * block)
    code = place + 256 * (coords[:, 0] % mine)

    outer = [(r, (r - 1) % rows if r % 2 == 0 else (r + 1) % rows) for r in range(rows)]
    partner = [(r, r ^ 1) for r in range(rows)]

    block_shape = jax.ShapeDtypeStruct((block, k, T), F32)
    gram_shape = jax.ShapeDtypeStruct((k // 2, 2 * k), F32)
    square = jax.ShapeDtypeStruct((k, k), F32)
    tbuf = pltpu.VMEM((cap, T, T), F32)
    panel = pltpu.VMEM((k, mine * T), F32)
    phl = pltpu.VMEM((mine, 2 * k, T), BF16)
    shl = pltpu.VMEM((3 * block + 1, 2 * k, T), BF16)
    acc = pltpu.VMEM((3 * block + 1, k, T), F32)
    img = pltpu.VMEM((mine, k, T), F32)
    sems = pltpu.SemaphoreType.DMA((cap // CHUNK,))

    def call(kernel, ins, outs, scratch, prefetch=0):
        return pl.pallas_call(
            kernel,
            grid_spec=pltpu.PrefetchScalarGridSpec(
                num_scalar_prefetch=prefetch, grid=(), in_specs=ins, out_specs=[VMEM] * len(outs), scratch_shapes=scratch
            ),
            out_shape=outs,
            compiler_params=pltpu.CompilerParams(vmem_limit_bytes=VMEM_LIMIT),
        )

    def over_grp(x):
        return lax.all_to_all(x, "grp", split_axis=0, concat_axis=0, tiled=True)

    def over_outer(x):
        return lax.ppermute(x, ROWS, outer)

    def over_partner(x):
        return lax.ppermute(x, ROWS, partner)

    def pieces(x):
        return x.reshape(groups, mine, k, T)

    def exchange(parts):
        p_outer, p_own, p_partner = parts
        total = p_own + over_outer(p_outer) + over_partner(p_partner)
        own = to_everyone(over_grp(pieces(total)).sum(axis=0), "grp").reshape(block, k, T)
        return over_outer(own), own, over_partner(own)

    def exchange_with_gram(parts, gram):
        p_outer, p_own, p_partner = parts
        gram = to_everyone(gram, ("z", "c"))
        got_outer = over_outer(p_outer)
        got = over_partner(p_partner)
        gram = gram.sum(axis=0)
        total = (p_own + got_outer + got).reshape(groups, mine * k, T)
        sides = jnp.broadcast_to(gram, (groups, *gram.shape))
        arrived = over_grp(jnp.concatenate([total, sides], axis=1)).sum(axis=0)
        middle, gram = arrived[: mine * k].reshape(mine, k, T), arrived[mine * k :]
        own = to_everyone(middle, "grp").reshape(block, k, T)
        own, gram = lax.optimization_barrier((own, gram))
        gram = to_everyone(gram, "y")
        at_outer = over_outer(own)
        at_partner = over_partner(own)
        return (at_outer, own, at_partner), gram

    def gram_parts(gram):
        gram = to_everyone(gram, ("c", "grp")).sum(axis=0)
        gram = to_everyone(gram, "z").sum(axis=0)
        return to_everyone(gram, "y")

    tile_halves = jax.ShapeDtypeStruct((cap, 2 * T, T), BF16)
    *parts, thl = call(
        first_kernel,
        [HBM, HBM],
        [block_shape] * 3 + [tile_halves],
        [tbuf, panel, phl, acc, sems, pltpu.SemaphoreType.DMA],
        2,
    )(code, live, tiles, sketch.T)
    whole = exchange(parts)
    *parts, gram = call(
        middle_kernel, [VMEM] * 4, [block_shape] * 3 + [gram_shape], [shl, img, phl, acc], 2
    )(code, live, thl, *whole)
    whole, gram = exchange_with_gram(parts, gram)
    linv = call(factor_kernel, [VMEM], [square], [], 0)(gram)[0]
    image, gram = call(
        last_kernel, [VMEM] * 5, [jax.ShapeDtypeStruct((k, mine * T), F32), gram_shape], [shl, img], 2
    )(code, live, thl, *whole, linv)
    scale = float(rows * groups * sketch.shape[0]) ** 0.5
    return call(
        functools.partial(basis_kernel, scale=scale), [VMEM] * 2, [jax.ShapeDtypeStruct(sketch.shape[::-1], F32)], [], 0
    )(gram_parts(gram), image)[0].T


def solution(mesh):
    finer = Mesh(mesh.devices.reshape(8, 8, 2, mesh.shape["grp"]), ROWS_GRP)
    placed = (P(ROWS_GRP, None, None), P(ROWS_GRP, None), P(ROWS_GRP), P(ROWS_GRP, None))
    return jax.shard_map(local, mesh=finer, in_specs=placed, out_specs=P(ROWS_GRP, None), check_vma=False)
```

```python
import functools

import jax
import jax.numpy as jnp
from jax import lax
from jax.experimental import pallas as pl
from jax.experimental.pallas import tpu as pltpu
from jax.sharding import Mesh
from jax.sharding import PartitionSpec as P


ROWS = ("y", "z", "c")
ROWS_GRP = ("y", "z", "c", "grp")
HIGHEST = lax.Precision.HIGHEST
F32 = jnp.float32
BF16 = jnp.bfloat16
T = 128
CHUNK = 8
VMEM_LIMIT = 50 * 1024 * 1024


def dot(a, b, contract, precision=None):
    return lax.dot_general(
        a, b, ((contract[:1], contract[1:]), ((), ())), precision=precision, preferred_element_type=F32
    )


def halves(x):
    hi = x.astype(BF16)
    return hi, (x - hi.astype(F32)).astype(BF16)


def fold(q, k):
    return (q[:k, :T] + q[k:, T:]) + (q[k:, :T] + q[:k, T:])


def tile_copy(c, tiles, tbuf, sems):
    at = pl.ds(c * CHUNK, CHUNK)
    return pltpu.make_async_copy(tiles.at[at], tbuf.at[at], sems.at[c])


def start_tiles(live, tiles, tbuf, sems):
    for c in range(tiles.shape[0] // CHUNK):

        @pl.when(c * CHUNK < live)
        def _():
            tile_copy(c, tiles, tbuf, sems).start()


def each_chunk(live, cap, work, ready=None):
    for c in range(cap // CHUNK):

        @pl.when(c * CHUNK < live)
        def _():
            if ready is not None:
                ready(c)
            for s in range(c * CHUNK, (c + 1) * CHUNK):
                work(s)


def keep_panel(panel, k, phl):
    for t in range(phl.shape[0]):
        hi, lo = halves(panel(t))
        phl[t, :k, :] = hi
        phl[t, k:, :] = lo


def spread_slot(entry, hi, lo, phl, acc):
    k = phl.shape[1] // 2
    at = entry & 255
    q = dot(phl[entry >> 8], jnp.concatenate([hi, lo], axis=1), (1, 0))
    acc[at] += fold(q, k)


def put_spread(acc, outs):
    each = outs[0].shape[0]
    for n, out in enumerate(outs):
        out[...] = acc[n * each : (n + 1) * each]


def slot_code(s, coords, live, block, mine, rows):
    odd = lax.axis_index("c")
    row = (lax.axis_index("y") * lax.axis_size("z") + lax.axis_index("z")) * 2 + odd
    column = coords[1, s]
    step = lax.rem(lax.div(column, block) - row + 1 + rows, rows)
    step = jnp.where(odd == 1, 2 - step, step)
    place = jnp.where(s < live, step * block + lax.rem(column, block), 3 * block)
    return place + 256 * lax.rem(coords[0, s], mine)


def first_kernel(
    coords, live, tiles, sketch, outer, own, partner, code, tbuf, panel, phl, acc, sems, panel_sem, *, rows
):
    cap = tiles.shape[0]
    k = sketch.shape[0]
    panel_copy = pltpu.make_async_copy(sketch, panel, panel_sem)
    panel_copy.start()
    start_tiles(live[0], tiles, tbuf, sems)
    acc[...] = jnp.zeros_like(acc)
    for s in range(cap):
        code[s] = slot_code(s, coords, live[0], outer.shape[0], phl.shape[0], rows)
    panel_copy.wait()
    keep_panel(lambda t: panel[:, t * T : (t + 1) * T], k, phl)
    each_chunk(
        live[0],
        cap,
        lambda s: spread_slot(code[s], *halves(tbuf[s]), phl, acc),
        lambda c: tile_copy(c, tiles, tbuf, sems).wait(),
    )
    put_spread(acc, (outer, own, partner))


def keep_spread(parts, shl):
    k = parts[0].shape[1]
    each = parts[0].shape[0]
    for n, part in enumerate(parts):

        def one(i, carry, part=part, n=n):
            hi, lo = halves(part[i])
            shl[n * each + i, :k, :] = hi
            shl[n * each + i, k:, :] = lo
            return carry

        lax.fori_loop(0, each, one, 0, unroll=4)
    shl[3 * each] = jnp.zeros_like(shl[3 * each])


def image_slot(entry, hi, lo, shl, img):
    k = shl.shape[1] // 2
    q = dot(shl[entry & 255], jnp.concatenate([hi, lo], axis=0), (1, 1))
    img[entry >> 8] += fold(q, k)


def whole_image(img):
    return jnp.concatenate([img[t] for t in range(img.shape[0])], axis=1)


def put_gram(image, out):
    g = dot(image, image, (1, 1), HIGHEST)
    h = g.shape[0] // 2
    quarters = (g[:h, :h], g[:h, h:], g[h:, h:])
    packed = jnp.concatenate(
        [jnp.concatenate([q[8 * r : 8 * r + 8] for r in range(h // 8)], axis=1) for q in quarters], axis=0
    )
    for n in range(out.shape[0]):
        out[n] = packed


def middle_kernel(
    code, live, tiles, s_outer, s_own, s_partner, outer, own, partner, gram,
    tbuf, thl, shl, img, phl, acc, sems,
):
    cap = tiles.shape[0]
    k = s_own.shape[1]
    start_tiles(live[0], tiles, tbuf, sems)
    keep_spread((s_outer, s_own, s_partner), shl)
    img[...] = jnp.zeros_like(img)
    acc[...] = jnp.zeros_like(acc)

    def forth(s):
        hi, lo = halves(tbuf[s])
        thl[s, :T, :] = hi
        thl[s, T:, :] = lo
        image_slot(code[s], hi, lo, shl, img)

    each_chunk(live[0], cap, forth, lambda c: tile_copy(c, tiles, tbuf, sems).wait())
    put_gram(whole_image(img), gram)
    keep_panel(lambda t: img[t], k, phl)
    each_chunk(live[0], cap, lambda s: spread_slot(code[s], thl[s, :T, :], thl[s, T:, :], phl, acc))
    put_spread(acc, (outer, own, partner))


def share_kernel(pieces, whole, gram):
    rows = whole.shape[1]
    total = pieces[0]
    for n in range(1, pieces.shape[0]):
        total = total + pieces[n]
    for n in range(whole.shape[0]):
        whole[n] = total[:rows]
    for n in range(gram.shape[0]):
        gram[n] = total[rows:]


def inverse_factor(g):
    k = g.shape[0]
    row_id = lax.broadcasted_iota(jnp.int32, (8, 2 * k), 0)
    eye = (lax.broadcasted_iota(jnp.int32, (k, k), 0) == lax.broadcasted_iota(jnp.int32, (k, k), 1)).astype(F32)
    full = jnp.concatenate([g, eye], axis=1)
    m = [full[8 * j : 8 * j + 8] for j in range(k // 8)]

    def row_of(x, r):
        return jnp.broadcast_to(x[r : r + 1, :], x.shape)

    for j in range(k // 8):
        rows = [row_of(m[j], t) for t in range(8)]
        cols = [
            {i: jnp.broadcast_to(m[i][:, 8 * j + t : 8 * j + t + 1], (8, 2 * k)) for i in range(j, k // 8)}
            for t in range(8)
        ]
        scale = jnp.zeros((8, 2 * k), F32)
        for t in range(8):
            pivot = row_of(cols[t][j], t)
            scale = jnp.where(row_id == t, lax.rsqrt(pivot), scale)
            inv = 1.0 / pivot
            q = rows[t] * inv
            cols[t][j] = jnp.where(row_id > t, cols[t][j], 0.0)
            for u in range(t + 1, 8):
                part = row_of(cols[t][j], u)
                f = part * inv
                rows[u] = rows[u] - part * q
                for i in range(j, k // 8):
                    cols[u][i] = cols[u][i] - cols[t][i] * f
            for i in range(j, k // 8):
                m[i] = m[i] - cols[t][i] * q
        m[j] = m[j] * scale
    return jnp.concatenate([x[:, k:] for x in m], axis=0)


def summed_gram(parts, k):
    packed = parts[0]
    for n in range(1, parts.shape[0]):
        packed = packed + parts[n]
    h = k // 2
    ul, ur, lr = (
        jnp.concatenate([packed[8 * q : 8 * q + 8, h * r : h * r + h] for r in range(h // 8)], axis=0) for q in range(3)
    )
    return jnp.concatenate([jnp.concatenate([ul, ur], axis=1), jnp.concatenate([ur.T, lr], axis=1)], axis=0)


def factor_kernel(parts, linv):
    linv[...] = inverse_factor(summed_gram(parts, linv.shape[0]))


def last_kernel(code, live, tiles, s_outer, s_own, s_partner, linv, image, gram, tbuf, shl, img, sems):
    start_tiles(live[0], tiles, tbuf, sems)
    keep_spread((s_outer, s_own, s_partner), shl)
    img[...] = jnp.zeros_like(img)
    each_chunk(
        live[0],
        tiles.shape[0],
        lambda s: image_slot(code[s], *halves(tbuf[s]), shl, img),
        lambda c: tile_copy(c, tiles, tbuf, sems).wait(),
    )
    x = dot(linv[...], whole_image(img), (1, 0), HIGHEST)
    image[...] = x
    put_gram(x, gram)


def basis_kernel(parts, image, basis, *, scale):
    linv = inverse_factor(summed_gram(parts, image.shape[0]))
    basis[...] = dot(linv, image[...], (1, 0), HIGHEST) * scale


def swapped(copies, axes):
    return lax.all_to_all(copies, axes, split_axis=0, concat_axis=0, tiled=True)


def to_everyone(x, axes):
    return swapped(jnp.broadcast_to(x, (lax.axis_size(axes), *x.shape)), axes)


VMEM = pl.BlockSpec(memory_space=pltpu.VMEM)
SMEM = pl.BlockSpec(memory_space=pltpu.SMEM)
HBM = pl.BlockSpec(memory_space=pltpu.HBM)


def call(kernel, ins, outs, scratch=(), prefetch=0, out_specs=None, limit=VMEM_LIMIT):
    return pl.pallas_call(
        kernel,
        grid_spec=pltpu.PrefetchScalarGridSpec(
            num_scalar_prefetch=prefetch,
            grid=(),
            in_specs=ins,
            out_specs=out_specs or [VMEM] * len(outs),
            scratch_shapes=scratch,
        ),
        out_shape=[jax.ShapeDtypeStruct(shape, dtype) for shape, dtype in outs],
        compiler_params=pltpu.CompilerParams(vmem_limit_bytes=limit),
    )


def local(tiles, coords, live, sketch):
    rows = lax.axis_size(ROWS)
    groups = lax.axis_size("grp")
    cap = tiles.shape[0]
    k = sketch.shape[1]
    mine = sketch.shape[0] // T
    block = groups * mine
    packed = (3 * 8, T)

    outer = [(r, (r - 1) % rows if r % 2 == 0 else (r + 1) % rows) for r in range(rows)]
    partner = [(r, r ^ 1) for r in range(rows)]

    tbuf = pltpu.VMEM((cap, T, T), F32)
    thl = pltpu.VMEM((cap, 2 * T, T), BF16)
    panel = pltpu.VMEM((k, mine * T), F32)
    phl = pltpu.VMEM((mine, 2 * k, T), BF16)
    shl = pltpu.VMEM((3 * block + 1, 2 * k, T), BF16)
    acc = pltpu.VMEM((3 * block + 1, k, T), F32)
    img = pltpu.VMEM((mine, k, T), F32)
    sems = pltpu.SemaphoreType.DMA((cap // CHUNK,))
    block_out = ((block, k, T), F32)

    def over_pairs(to_outer, to_partner):
        got_outer = lax.ppermute(to_outer, ROWS, outer)
        got_partner = lax.ppermute(to_partner, ROWS, partner)
        return got_outer, got_partner

    def pieces(x):
        return x.reshape(groups, mine * k, T)

    def exchange(parts):
        p_outer, p_own, p_partner = parts
        got_outer, got = over_pairs(p_outer, p_partner)
        total = p_own + got_outer + got
        own = to_everyone(swapped(pieces(total), "grp").sum(axis=0), "grp").reshape(block, k, T)
        at_outer, at_partner = over_pairs(own, own)
        return at_outer, own, at_partner

    def exchange_with_gram(parts, gram):
        p_outer, p_own, p_partner = parts
        gram = swapped(gram, ("z", "c"))
        got_outer, got = over_pairs(p_outer, p_partner)
        total = pieces(p_own + got_outer + got)
        sides = jnp.broadcast_to(gram.sum(axis=0), (groups, *packed))
        arrived = swapped(jnp.concatenate([total, sides], axis=1), "grp")
        copies, gram = call(
            share_kernel, [VMEM], [((groups, mine * k, T), F32), ((lax.axis_size("y"), *packed), F32)]
        )(arrived)
        own = swapped(copies, "grp").reshape(block, k, T)
        own, gram = lax.optimization_barrier((own, gram))
        gram = swapped(gram, "y")
        at_outer, at_partner = over_pairs(own, own)
        return (at_outer, own, at_partner), gram

    *parts, code = call(
        functools.partial(first_kernel, rows=rows),
        [HBM, HBM],
        [block_out] * 3 + [((cap,), jnp.int32)],
        [tbuf, panel, phl, acc, sems, pltpu.SemaphoreType.DMA],
        2,
        [VMEM] * 3 + [SMEM],
    )(coords.T, live, tiles, sketch.T)
    whole = exchange(parts)
    *parts, gram = call(
        middle_kernel,
        [HBM] + [VMEM] * 3,
        [block_out] * 3 + [((2 * lax.axis_size("z"), *packed), F32)],
        [tbuf, thl, shl, img, phl, acc, sems],
        2,
    )(code, live, tiles, *whole)
    whole, gram = exchange_with_gram(parts, gram)
    linv = call(factor_kernel, [VMEM], [((k, k), F32)])(gram)[0]
    image, gram = call(
        last_kernel, [HBM] + [VMEM] * 4, [((k, mine * T), F32), ((2 * groups, *packed), F32)], [tbuf, shl, img, sems], 2
    )(code, live, tiles, *whole, linv)
    gram = to_everyone(swapped(gram, ("c", "grp")).sum(axis=0), "z").sum(axis=0)
    scale = float(rows * groups * sketch.shape[0]) ** 0.5
    return call(
        functools.partial(basis_kernel, scale=scale), [VMEM] * 2, [(sketch.shape[::-1], F32)]
    )(to_everyone(gram, "y"), image)[0].T


def solution(mesh):
    finer = Mesh(mesh.devices.reshape(8, 8, 2, mesh.shape["grp"]), ROWS_GRP)
    placed = (P(ROWS_GRP, None, None), P(ROWS_GRP, None), P(ROWS_GRP), P(ROWS_GRP, None))
    return jax.shard_map(local, mesh=finer, in_specs=placed, out_specs=P(ROWS_GRP, None), check_vma=False)
```

```python
import functools

import jax
import jax.numpy as jnp
from jax import lax
from jax.experimental import pallas as pl
from jax.experimental.pallas import tpu as pltpu
from jax.sharding import Mesh
from jax.sharding import PartitionSpec as P


ROWS = ("y", "z", "c")
ROWS_GRP = ("y", "z", "c", "grp")
HIGHEST = lax.Precision.HIGHEST
F32 = jnp.float32
BF16 = jnp.bfloat16
T = 128
CHUNK = 8
VMEM_LIMIT = 50 * 1024 * 1024


def dot(a, b, contract, precision=None):
    return lax.dot_general(
        a, b, ((contract[:1], contract[1:]), ((), ())), precision=precision, preferred_element_type=F32
    )


def halves(x):
    hi = x.astype(BF16)
    return hi, (x - hi.astype(F32)).astype(BF16)


def fold(q, k):
    return (q[:k, :T] + q[k:, T:]) + (q[k:, :T] + q[:k, T:])


def tile_copy(c, tiles, tbuf, sems):
    at = pl.ds(c * CHUNK, CHUNK)
    return pltpu.make_async_copy(tiles.at[at], tbuf.at[at], sems.at[c])


def start_tiles(live, tiles, tbuf, sems):
    for c in range(tiles.shape[0] // CHUNK):

        @pl.when(c * CHUNK < live)
        def _():
            tile_copy(c, tiles, tbuf, sems).start()


def each_chunk(live, cap, work, ready=None):
    for c in range(cap // CHUNK):

        @pl.when(c * CHUNK < live)
        def _():
            if ready is not None:
                ready(c)
            for s in range(c * CHUNK, (c + 1) * CHUNK):
                work(s)


def keep_panel(panel, k, phl):
    for t in range(phl.shape[0]):
        hi, lo = halves(panel(t))
        phl[t, :k, :] = hi
        phl[t, k:, :] = lo


def spread_slot(entry, hi, lo, phl, acc):
    k = phl.shape[1] // 2
    at = entry & 255
    q = dot(phl[entry >> 8], jnp.concatenate([hi, lo], axis=1), (1, 0))
    acc[at] += fold(q, k)


def put_spread(acc, outs):
    each = outs[0].shape[0]
    for n, out in enumerate(outs):
        out[...] = acc[n * each : (n + 1) * each]


def slot_code(s, coords, live, block, mine, rows):
    odd = lax.axis_index("c")
    row = (lax.axis_index("y") * lax.axis_size("z") + lax.axis_index("z")) * 2 + odd
    column = coords[1, s]
    step = lax.rem(lax.div(column, block) - row + 1 + rows, rows)
    step = jnp.where(odd == 1, 2 - step, step)
    place = jnp.where(s < live, step * block + lax.rem(column, block), 3 * block)
    return place + 256 * lax.rem(coords[0, s], mine)


def first_kernel(
    coords, live, tiles, sketch, outer, own, partner, code, tbuf, panel, phl, acc, sems, panel_sem, *, rows
):
    cap = tiles.shape[0]
    k = sketch.shape[0]
    panel_copy = pltpu.make_async_copy(sketch, panel, panel_sem)
    panel_copy.start()
    start_tiles(live[0], tiles, tbuf, sems)
    acc[...] = jnp.zeros_like(acc)
    for s in range(cap):
        code[s] = slot_code(s, coords, live[0], outer.shape[0], phl.shape[0], rows)
    panel_copy.wait()
    keep_panel(lambda t: panel[:, t * T : (t + 1) * T], k, phl)
    each_chunk(
        live[0],
        cap,
        lambda s: spread_slot(code[s], *halves(tbuf[s]), phl, acc),
        lambda c: tile_copy(c, tiles, tbuf, sems).wait(),
    )
    put_spread(acc, (outer, own, partner))


def keep_spread(parts, shl):
    k = parts[0].shape[1]
    each = parts[0].shape[0]
    for n, part in enumerate(parts):

        def one(i, carry, part=part, n=n):
            hi, lo = halves(part[i])
            shl[n * each + i, :k, :] = hi
            shl[n * each + i, k:, :] = lo
            return carry

        lax.fori_loop(0, each, one, 0, unroll=4)
    shl[3 * each] = jnp.zeros_like(shl[3 * each])


def image_slot(entry, hi, lo, shl, img):
    k = shl.shape[1] // 2
    q = dot(shl[entry & 255], jnp.concatenate([hi, lo], axis=0), (1, 1))
    img[entry >> 8] += fold(q, k)


def whole_image(img):
    return jnp.concatenate([img[t] for t in range(img.shape[0])], axis=1)


def put_gram(image, out):
    g = dot(image, image, (1, 1), HIGHEST)
    h = g.shape[0] // 2
    quarters = (g[:h, :h], g[:h, h:], g[h:, h:])
    packed = jnp.concatenate(
        [jnp.concatenate([q[8 * r : 8 * r + 8] for r in range(h // 8)], axis=1) for q in quarters], axis=0
    )
    for n in range(out.shape[0]):
        out[n] = packed


def middle_kernel(
    code, live, tiles, s_outer, s_own, s_partner, outer, own, partner, gram,
    tbuf, thl, shl, img, phl, acc, sems,
):
    cap = tiles.shape[0]
    k = s_own.shape[1]
    start_tiles(live[0], tiles, tbuf, sems)
    keep_spread((s_outer, s_own, s_partner), shl)
    img[...] = jnp.zeros_like(img)
    acc[...] = jnp.zeros_like(acc)

    def forth(s):
        hi, lo = halves(tbuf[s])
        thl[s, :T, :] = hi
        thl[s, T:, :] = lo
        image_slot(code[s], hi, lo, shl, img)

    each_chunk(live[0], cap, forth, lambda c: tile_copy(c, tiles, tbuf, sems).wait())
    put_gram(whole_image(img), gram)
    keep_panel(lambda t: img[t], k, phl)
    each_chunk(live[0], cap, lambda s: spread_slot(code[s], thl[s, :T, :], thl[s, T:, :], phl, acc))
    put_spread(acc, (outer, own, partner))


def share_kernel(pieces, whole, gram):
    rows = whole.shape[1]
    total = pieces[0]
    for n in range(1, pieces.shape[0]):
        total = total + pieces[n]
    for n in range(whole.shape[0]):
        whole[n] = total[:rows]
    for n in range(gram.shape[0]):
        gram[n] = total[rows:]


def inverse_factor(g):
    k = g.shape[0]
    row_id = lax.broadcasted_iota(jnp.int32, (8, 2 * k), 0)
    eye = (lax.broadcasted_iota(jnp.int32, (k, k), 0) == lax.broadcasted_iota(jnp.int32, (k, k), 1)).astype(F32)
    full = jnp.concatenate([g, eye], axis=1)
    m = [full[8 * j : 8 * j + 8] for j in range(k // 8)]

    def row_of(x, r):
        return jnp.broadcast_to(x[r : r + 1, :], x.shape)

    for j in range(k // 8):
        rows = [row_of(m[j], t) for t in range(8)]
        cols = [
            {i: jnp.broadcast_to(m[i][:, 8 * j + t : 8 * j + t + 1], (8, 2 * k)) for i in range(j, k // 8)}
            for t in range(8)
        ]
        scale = jnp.zeros((8, 2 * k), F32)
        for t in range(8):
            pivot = row_of(cols[t][j], t)
            scale = jnp.where(row_id == t, lax.rsqrt(pivot), scale)
            inv = 1.0 / pivot
            q = rows[t] * inv
            cols[t][j] = jnp.where(row_id > t, cols[t][j], 0.0)
            for u in range(t + 1, 8):
                part = row_of(cols[t][j], u)
                f = part * inv
                rows[u] = rows[u] - part * q
                for i in range(j, k // 8):
                    cols[u][i] = cols[u][i] - cols[t][i] * f
            for i in range(j, k // 8):
                m[i] = m[i] - cols[t][i] * q
        m[j] = m[j] * scale
    return jnp.concatenate([x[:, k:] for x in m], axis=0)


def summed_gram(parts, k):
    packed = parts[0]
    for n in range(1, parts.shape[0]):
        packed = packed + parts[n]
    h = k // 2
    ul, ur, lr = (
        jnp.concatenate([packed[8 * q : 8 * q + 8, h * r : h * r + h] for r in range(h // 8)], axis=0) for q in range(3)
    )
    return jnp.concatenate([jnp.concatenate([ul, ur], axis=1), jnp.concatenate([ur.T, lr], axis=1)], axis=0)


def factor_kernel(parts, linv):
    linv[...] = inverse_factor(summed_gram(parts, linv.shape[0]))


def last_kernel(code, live, tiles, s_outer, s_own, s_partner, linv, image, gram, tbuf, shl, img, sems):
    start_tiles(live[0], tiles, tbuf, sems)
    keep_spread((s_outer, s_own, s_partner), shl)
    img[...] = jnp.zeros_like(img)
    each_chunk(
        live[0],
        tiles.shape[0],
        lambda s: image_slot(code[s], *halves(tbuf[s]), shl, img),
        lambda c: tile_copy(c, tiles, tbuf, sems).wait(),
    )
    x = dot(linv[...], whole_image(img), (1, 0), HIGHEST)
    image[...] = x
    put_gram(x, gram)


def basis_kernel(parts, image, basis, *, scale):
    linv = inverse_factor(summed_gram(parts, image.shape[0]))
    basis[...] = dot(linv, image[...], (1, 0), HIGHEST) * scale


def swapped(copies, axes):
    return lax.all_to_all(copies, axes, split_axis=0, concat_axis=0, tiled=True)


in_space = pltpu.with_memory_space_constraint


def to_everyone(x, axes):
    return swapped(jnp.broadcast_to(x, (lax.axis_size(axes), *x.shape)), axes)


VMEM = pl.BlockSpec(memory_space=pltpu.VMEM)
SMEM = pl.BlockSpec(memory_space=pltpu.SMEM)
HBM = pl.BlockSpec(memory_space=pltpu.HBM)


def call(kernel, ins, outs, scratch=(), prefetch=0, out_specs=None, limit=VMEM_LIMIT):
    return pl.pallas_call(
        kernel,
        grid_spec=pltpu.PrefetchScalarGridSpec(
            num_scalar_prefetch=prefetch,
            grid=(),
            in_specs=ins,
            out_specs=out_specs or [VMEM] * len(outs),
            scratch_shapes=scratch,
        ),
        out_shape=[jax.ShapeDtypeStruct(shape, dtype) for shape, dtype in outs],
        compiler_params=pltpu.CompilerParams(vmem_limit_bytes=limit),
    )


def local(tiles, coords, live, sketch):
    rows = lax.axis_size(ROWS)
    groups = lax.axis_size("grp")
    cap = tiles.shape[0]
    k = sketch.shape[1]
    mine = sketch.shape[0] // T
    block = groups * mine
    packed = (3 * 8, T)

    outer = [(r, (r - 1) % rows if r % 2 == 0 else (r + 1) % rows) for r in range(rows)]
    partner = [(r, r ^ 1) for r in range(rows)]

    tbuf = pltpu.VMEM((cap, T, T), F32)
    thl = pltpu.VMEM((cap, 2 * T, T), BF16)
    panel = pltpu.VMEM((k, mine * T), F32)
    phl = pltpu.VMEM((mine, 2 * k, T), BF16)
    shl = pltpu.VMEM((3 * block + 1, 2 * k, T), BF16)
    acc = pltpu.VMEM((3 * block + 1, k, T), F32)
    img = pltpu.VMEM((mine, k, T), F32)
    sems = pltpu.SemaphoreType.DMA((cap // CHUNK,))
    block_out = ((block, k, T), F32)

    def over_pairs(to_outer, to_partner):
        got_outer = lax.ppermute(to_outer, ROWS, outer)
        got_partner = lax.ppermute(to_partner, ROWS, partner)
        return got_outer, got_partner

    def pieces(x):
        return x.reshape(groups, mine * k, T)

    def exchange(parts):
        p_outer, p_own, p_partner = parts
        got_outer, got = over_pairs(p_outer, p_partner)
        total = p_own + got_outer + got
        own = to_everyone(swapped(pieces(total), "grp").sum(axis=0), "grp").reshape(block, k, T)
        at_outer, at_partner = over_pairs(own, own)
        return at_outer, own, at_partner

    def exchange_with_gram(parts, gram):
        p_outer, p_own, p_partner = parts
        gram = swapped(gram, ("y", "c"))
        got_outer, got = over_pairs(p_outer, p_partner)
        total = pieces(p_own + got_outer + got)
        sides = jnp.broadcast_to(gram.sum(axis=0), (groups, *packed))
        arrived = swapped(jnp.concatenate([total, sides], axis=1), "grp")
        copies, gram = call(
            share_kernel, [VMEM], [((groups, mine * k, T), F32), ((lax.axis_size("z"), *packed), F32)]
        )(arrived)
        own = swapped(copies, "grp").reshape(block, k, T)
        own, gram = lax.optimization_barrier((own, gram))
        gram = swapped(gram, "z")
        at_outer, at_partner = over_pairs(own, own)
        return (at_outer, own, at_partner), gram

    *parts, code = call(
        functools.partial(first_kernel, rows=rows),
        [HBM, HBM],
        [block_out] * 3 + [((cap,), jnp.int32)],
        [tbuf, panel, phl, acc, sems, pltpu.SemaphoreType.DMA],
        2,
        [VMEM] * 3 + [SMEM],
    )(in_space(coords.T, pltpu.HBM), live, tiles, in_space(sketch.T, pltpu.HBM))
    whole = exchange(parts)
    *parts, gram = call(
        middle_kernel,
        [HBM] + [VMEM] * 3,
        [block_out] * 3 + [((2 * lax.axis_size("y"), *packed), F32)],
        [tbuf, thl, shl, img, phl, acc, sems],
        2,
    )(code, live, tiles, *whole)
    whole, gram = exchange_with_gram(parts, gram)
    linv = call(factor_kernel, [VMEM], [((k, k), F32)])(gram)[0]
    image, gram = call(
        last_kernel, [HBM] + [VMEM] * 4, [((k, mine * T), F32), ((2 * groups, *packed), F32)], [tbuf, shl, img, sems], 2
    )(code, live, tiles, *whole, linv)
    gram = to_everyone(swapped(gram, ("c", "grp")).sum(axis=0), "z").sum(axis=0)
    scale = float(rows * groups * sketch.shape[0]) ** 0.5
    return call(
        functools.partial(basis_kernel, scale=scale), [VMEM] * 2, [(sketch.shape[::-1], F32)]
    )(to_everyone(gram, "y"), image)[0].T


def solution(mesh):
    finer = Mesh(mesh.devices.reshape(8, 8, 2, mesh.shape["grp"]), ROWS_GRP)
    placed = (P(ROWS_GRP, None, None), P(ROWS_GRP, None), P(ROWS_GRP), P(ROWS_GRP, None))
    return jax.shard_map(local, mesh=finer, in_specs=placed, out_specs=P(ROWS_GRP, None), check_vma=False)
```

```python
import functools

import jax
import jax.numpy as jnp
from jax import lax
from jax.experimental import pallas as pl
from jax.experimental.pallas import tpu as pltpu
from jax.sharding import Mesh
from jax.sharding import PartitionSpec as P


ROWS = ("y", "z", "c")
ROWS_GRP = ("y", "z", "c", "grp")
HIGHEST = lax.Precision.HIGHEST
F32 = jnp.float32
BF16 = jnp.bfloat16
T = 128
CHUNK = 8
VMEM_LIMIT = 50 * 1024 * 1024


def dot(a, b, contract, precision=None):
    return lax.dot_general(
        a, b, ((contract[:1], contract[1:]), ((), ())), precision=precision, preferred_element_type=F32
    )


def halves(x):
    hi = x.astype(BF16)
    return hi, (x - hi.astype(F32)).astype(BF16)


def fold(q, k):
    return (q[:k, :T] + q[k:, T:]) + (q[k:, :T] + q[:k, T:])


def tile_copy(c, tiles, tbuf, sems):
    at = pl.ds(c * CHUNK, CHUNK)
    return pltpu.make_async_copy(tiles.at[at], tbuf.at[at], sems.at[c])


def start_tiles(live, tiles, tbuf, sems):
    for c in range(tiles.shape[0] // CHUNK):

        @pl.when(c * CHUNK < live)
        def _():
            tile_copy(c, tiles, tbuf, sems).start()


def each_chunk(live, cap, work, ready=None):
    for c in range(cap // CHUNK):

        @pl.when(c * CHUNK < live)
        def _():
            if ready is not None:
                ready(c)
            for s in range(c * CHUNK, (c + 1) * CHUNK):
                work(s)


def keep_panel(panel, k, phl):
    for t in range(phl.shape[0]):
        hi, lo = halves(panel(t))
        phl[t, :k, :] = hi
        phl[t, k:, :] = lo


def spread_slot(entry, hi, lo, phl, acc):
    k = phl.shape[1] // 2
    at = entry & 255
    q = dot(phl[entry >> 8], jnp.concatenate([hi, lo], axis=1), (1, 0))
    acc[at] += fold(q, k)


def put_spread(acc, outs):
    each = outs[0].shape[0]
    for n, out in enumerate(outs):
        out[...] = acc[n * each : (n + 1) * each]


def slot_code(s, coords, live, block, mine, rows):
    odd = lax.axis_index("c")
    row = (lax.axis_index("y") * lax.axis_size("z") + lax.axis_index("z")) * 2 + odd
    column = coords[1, s]
    step = lax.rem(lax.div(column, block) - row + 1 + rows, rows)
    step = jnp.where(odd == 1, 2 - step, step)
    place = jnp.where(s < live, step * block + lax.rem(column, block), 3 * block)
    return place + 256 * lax.rem(coords[0, s], mine)


def first_kernel(
    coords, live, tiles, sketch, outer, own, partner, code, tbuf, panel, phl, acc, sems, panel_sem, *, rows
):
    cap = tiles.shape[0]
    k = sketch.shape[0]
    panel_copy = pltpu.make_async_copy(sketch, panel, panel_sem)
    panel_copy.start()
    start_tiles(live[0], tiles, tbuf, sems)
    acc[...] = jnp.zeros_like(acc)
    for s in range(cap):
        code[s] = slot_code(s, coords, live[0], outer.shape[0], phl.shape[0], rows)
    panel_copy.wait()
    keep_panel(lambda t: panel[:, t * T : (t + 1) * T], k, phl)
    each_chunk(
        live[0],
        cap,
        lambda s: spread_slot(code[s], *halves(tbuf[s]), phl, acc),
        lambda c: tile_copy(c, tiles, tbuf, sems).wait(),
    )
    put_spread(acc, (outer, own, partner))


def keep_spread(parts, shl):
    k = parts[0].shape[1]
    each = parts[0].shape[0]
    for n, part in enumerate(parts):

        def one(i, carry, part=part, n=n):
            hi, lo = halves(part[i])
            shl[n * each + i, :k, :] = hi
            shl[n * each + i, k:, :] = lo
            return carry

        lax.fori_loop(0, each, one, 0, unroll=4)
    shl[3 * each] = jnp.zeros_like(shl[3 * each])


def image_slot(entry, hi, lo, shl, img):
    k = shl.shape[1] // 2
    q = dot(shl[entry & 255], jnp.concatenate([hi, lo], axis=0), (1, 1))
    img[entry >> 8] += fold(q, k)


def whole_image(img):
    return jnp.concatenate([img[t] for t in range(img.shape[0])], axis=1)


def put_gram(image, out):
    g = dot(image, image, (1, 1), HIGHEST)
    h = g.shape[0] // 2
    quarters = (g[:h, :h], g[:h, h:], g[h:, h:])
    packed = jnp.concatenate(
        [jnp.concatenate([q[8 * r : 8 * r + 8] for r in range(h // 8)], axis=1) for q in quarters], axis=0
    )
    for n in range(out.shape[0]):
        out[n] = packed


def middle_kernel(
    code, live, tiles, s_outer, s_own, s_partner, outer, own, partner, gram,
    tbuf, thl, shl, img, phl, acc, sems,
):
    cap = tiles.shape[0]
    k = s_own.shape[1]
    start_tiles(live[0], tiles, tbuf, sems)
    keep_spread((s_outer, s_own, s_partner), shl)
    img[...] = jnp.zeros_like(img)
    acc[...] = jnp.zeros_like(acc)

    def forth(s):
        hi, lo = halves(tbuf[s])
        thl[s, :T, :] = hi
        thl[s, T:, :] = lo
        image_slot(code[s], hi, lo, shl, img)

    each_chunk(live[0], cap, forth, lambda c: tile_copy(c, tiles, tbuf, sems).wait())
    put_gram(whole_image(img), gram)
    keep_panel(lambda t: img[t], k, phl)
    each_chunk(live[0], cap, lambda s: spread_slot(code[s], thl[s, :T, :], thl[s, T:, :], phl, acc))
    put_spread(acc, (outer, own, partner))


def share_kernel(pieces, whole, gram):
    rows = whole.shape[1]
    total = pieces[0]
    for n in range(1, pieces.shape[0]):
        total = total + pieces[n]
    for n in range(whole.shape[0]):
        whole[n] = total[:rows]
    gram[...] = total[rows:]


def inverse_factor(g):
    k = g.shape[0]
    row_id = lax.broadcasted_iota(jnp.int32, (8, 2 * k), 0)
    eye = (lax.broadcasted_iota(jnp.int32, (k, k), 0) == lax.broadcasted_iota(jnp.int32, (k, k), 1)).astype(F32)
    full = jnp.concatenate([g, eye], axis=1)
    m = [full[8 * j : 8 * j + 8] for j in range(k // 8)]

    def row_of(x, r):
        return jnp.broadcast_to(x[r : r + 1, :], x.shape)

    for j in range(k // 8):
        rows = [row_of(m[j], t) for t in range(8)]
        cols = [
            {i: jnp.broadcast_to(m[i][:, 8 * j + t : 8 * j + t + 1], (8, 2 * k)) for i in range(j, k // 8)}
            for t in range(8)
        ]
        scale = jnp.zeros((8, 2 * k), F32)
        for t in range(8):
            pivot = row_of(cols[t][j], t)
            scale = jnp.where(row_id == t, lax.rsqrt(pivot), scale)
            inv = 1.0 / pivot
            q = rows[t] * inv
            cols[t][j] = jnp.where(row_id > t, cols[t][j], 0.0)
            for u in range(t + 1, 8):
                part = row_of(cols[t][j], u)
                f = part * inv
                rows[u] = rows[u] - part * q
                for i in range(j, k // 8):
                    cols[u][i] = cols[u][i] - cols[t][i] * f
            for i in range(j, k // 8):
                m[i] = m[i] - cols[t][i] * q
        m[j] = m[j] * scale
    return jnp.concatenate([x[:, k:] for x in m], axis=0)


def summed_gram(parts, k):
    packed = parts[0]
    for n in range(1, parts.shape[0]):
        packed = packed + parts[n]
    h = k // 2
    ul, ur, lr = (
        jnp.concatenate([packed[8 * q : 8 * q + 8, h * r : h * r + h] for r in range(h // 8)], axis=0) for q in range(3)
    )
    return jnp.concatenate([jnp.concatenate([ul, ur], axis=1), jnp.concatenate([ur.T, lr], axis=1)], axis=0)


def factor_kernel(parts, linv):
    linv[...] = inverse_factor(summed_gram(parts, linv.shape[0]))


def last_kernel(code, live, tiles, s_outer, s_own, s_partner, linv, image, gram, tbuf, shl, img, sems):
    start_tiles(live[0], tiles, tbuf, sems)
    keep_spread((s_outer, s_own, s_partner), shl)
    img[...] = jnp.zeros_like(img)
    each_chunk(
        live[0],
        tiles.shape[0],
        lambda s: image_slot(code[s], *halves(tbuf[s]), shl, img),
        lambda c: tile_copy(c, tiles, tbuf, sems).wait(),
    )
    x = dot(linv[...], whole_image(img), (1, 0), HIGHEST)
    image[...] = x
    put_gram(x, gram)


def basis_kernel(parts, image, basis, *, scale):
    linv = inverse_factor(summed_gram(parts, image.shape[0]))
    basis[...] = dot(linv, image[...], (1, 0), HIGHEST) * scale


def swapped(copies, axes):
    return lax.all_to_all(copies, axes, split_axis=0, concat_axis=0, tiled=True)


in_space = pltpu.with_memory_space_constraint


def to_everyone(x, axes):
    return swapped(jnp.broadcast_to(x, (lax.axis_size(axes), *x.shape)), axes)


VMEM = pl.BlockSpec(memory_space=pltpu.VMEM)
SMEM = pl.BlockSpec(memory_space=pltpu.SMEM)
HBM = pl.BlockSpec(memory_space=pltpu.HBM)


def call(kernel, ins, outs, scratch=(), prefetch=0, out_specs=None, limit=VMEM_LIMIT):
    return pl.pallas_call(
        kernel,
        grid_spec=pltpu.PrefetchScalarGridSpec(
            num_scalar_prefetch=prefetch,
            grid=(),
            in_specs=ins,
            out_specs=out_specs or [VMEM] * len(outs),
            scratch_shapes=scratch,
        ),
        out_shape=[jax.ShapeDtypeStruct(shape, dtype) for shape, dtype in outs],
        compiler_params=pltpu.CompilerParams(vmem_limit_bytes=limit),
    )


def local(tiles, coords, live, sketch):
    rows = lax.axis_size(ROWS)
    groups = lax.axis_size("grp")
    cap = tiles.shape[0]
    k = sketch.shape[1]
    mine = sketch.shape[0] // T
    block = groups * mine
    packed = (3 * 8, T)

    outer = [(r, (r - 1) % rows if r % 2 == 0 else (r + 1) % rows) for r in range(rows)]
    partner = [(r, r ^ 1) for r in range(rows)]

    tbuf = pltpu.VMEM((cap, T, T), F32)
    thl = pltpu.VMEM((cap, 2 * T, T), BF16)
    panel = pltpu.VMEM((k, mine * T), F32)
    phl = pltpu.VMEM((mine, 2 * k, T), BF16)
    shl = pltpu.VMEM((3 * block + 1, 2 * k, T), BF16)
    acc = pltpu.VMEM((3 * block + 1, k, T), F32)
    img = pltpu.VMEM((mine, k, T), F32)
    sems = pltpu.SemaphoreType.DMA((cap // CHUNK,))
    block_out = ((block, k, T), F32)

    def over_pairs(to_outer, to_partner):
        got_outer = lax.ppermute(to_outer, ROWS, outer)
        got_partner = lax.ppermute(to_partner, ROWS, partner)
        return got_outer, got_partner

    def pieces(x):
        return x.reshape(groups, mine * k, T)

    def exchange(parts):
        p_outer, p_own, p_partner = parts
        got_outer, got = over_pairs(p_outer, p_partner)
        total = p_own + got_outer + got
        own = to_everyone(swapped(pieces(total), "grp").sum(axis=0), "grp").reshape(block, k, T)
        at_outer, at_partner = over_pairs(own, own)
        return at_outer, own, at_partner

    def exchange_with_gram(parts, gram):
        p_outer, p_own, p_partner = parts
        gram = swapped(gram, "y")
        got_outer, got = over_pairs(p_outer, p_partner)
        total = pieces(p_own + got_outer + got)
        sides = jnp.broadcast_to(gram.sum(axis=0), (groups, *packed))
        arrived = swapped(jnp.concatenate([total, sides], axis=1), "grp")
        copies, gram = call(share_kernel, [VMEM], [((groups, mine * k, T), F32), (packed, F32)])(arrived)
        own = swapped(copies, "grp").reshape(block, k, T)
        beside = lax.ppermute(gram, ROWS, partner)
        own, gram = lax.optimization_barrier((own, gram + beside))
        gram = to_everyone(gram, "z")
        at_outer, at_partner = over_pairs(own, own)
        return (at_outer, own, at_partner), gram

    *parts, code = call(
        functools.partial(first_kernel, rows=rows),
        [HBM, HBM],
        [block_out] * 3 + [((cap,), jnp.int32)],
        [tbuf, panel, phl, acc, sems, pltpu.SemaphoreType.DMA],
        2,
        [VMEM] * 3 + [SMEM],
    )(in_space(coords.T, pltpu.HBM), live, tiles, in_space(sketch.T, pltpu.HBM))
    whole = exchange(parts)
    *parts, gram = call(
        middle_kernel,
        [HBM] + [VMEM] * 3,
        [block_out] * 3 + [((lax.axis_size("y"), *packed), F32)],
        [tbuf, thl, shl, img, phl, acc, sems],
        2,
    )(code, live, tiles, *whole)
    whole, gram = exchange_with_gram(parts, gram)
    linv = call(factor_kernel, [VMEM], [((k, k), F32)])(gram)[0]
    image, gram = call(
        last_kernel, [HBM] + [VMEM] * 4, [((k, mine * T), F32), ((2 * groups, *packed), F32)], [tbuf, shl, img, sems], 2
    )(code, live, tiles, *whole, linv)
    gram = to_everyone(swapped(gram, ("c", "grp")).sum(axis=0), "z").sum(axis=0)
    scale = float(rows * groups * sketch.shape[0]) ** 0.5
    return call(
        functools.partial(basis_kernel, scale=scale), [VMEM] * 2, [(sketch.shape[::-1], F32)]
    )(to_everyone(gram, "y"), image)[0].T


def solution(mesh):
    finer = Mesh(mesh.devices.reshape(8, 8, 2, mesh.shape["grp"]), ROWS_GRP)
    placed = (P(ROWS_GRP, None, None), P(ROWS_GRP, None), P(ROWS_GRP), P(ROWS_GRP, None))
    return jax.shard_map(local, mesh=finer, in_specs=placed, out_specs=P(ROWS_GRP, None), check_vma=False)
```

```python
import functools

import jax
import jax.numpy as jnp
from jax import lax
from jax.experimental import pallas as pl
from jax.experimental.pallas import tpu as pltpu
from jax.sharding import Mesh
from jax.sharding import PartitionSpec as P


ROWS = ("y", "z", "c")
ROWS_GRP = ("y", "z", "c", "grp")
HIGHEST = lax.Precision.HIGHEST
F32 = jnp.float32
BF16 = jnp.bfloat16
T = 128
CHUNK = 8
VMEM_LIMIT = 50 * 1024 * 1024


def dot(a, b, contract, precision=None):
    return lax.dot_general(
        a, b, ((contract[:1], contract[1:]), ((), ())), precision=precision, preferred_element_type=F32
    )


def halves(x):
    hi = x.astype(BF16)
    return hi, (x - hi.astype(F32)).astype(BF16)


def fold(q, k):
    return (q[:k, :T] + q[k:, T:]) + (q[k:, :T] + q[:k, T:])


def tile_copy(c, tiles, tbuf, sems):
    at = pl.ds(c * CHUNK, CHUNK)
    return pltpu.make_async_copy(tiles.at[at], tbuf.at[at], sems.at[c])


def start_tiles(live, tiles, tbuf, sems):
    for c in range(tiles.shape[0] // CHUNK):

        @pl.when(c * CHUNK < live)
        def _():
            tile_copy(c, tiles, tbuf, sems).start()


def each_chunk(live, cap, work, ready=None):
    for c in range(cap // CHUNK):

        @pl.when(c * CHUNK < live)
        def _():
            if ready is not None:
                ready(c)
            for s in range(c * CHUNK, (c + 1) * CHUNK):
                work(s)


def keep_panel(panel, k, phl):
    for t in range(phl.shape[0]):
        hi, lo = halves(panel(t))
        phl[t, :k, :] = hi
        phl[t, k:, :] = lo


def spread_slot(entry, hi, lo, phl, acc):
    k = phl.shape[1] // 2
    at = entry & 255
    q = dot(phl[entry >> 8], jnp.concatenate([hi, lo], axis=1), (1, 0))
    acc[at] += fold(q, k)


def put_spread(acc, outs):
    each = outs[0].shape[0]
    for n, out in enumerate(outs):
        out[...] = acc[n * each : (n + 1) * each]


def slot_code(s, coords, live, block, mine, rows):
    odd = lax.axis_index("c")
    row = (lax.axis_index("y") * lax.axis_size("z") + lax.axis_index("z")) * 2 + odd
    column = coords[1, s]
    step = lax.rem(lax.div(column, block) - row + 1 + rows, rows)
    step = jnp.where(odd == 1, 2 - step, step)
    place = jnp.where(s < live, step * block + lax.rem(column, block), 3 * block)
    return place + 256 * lax.rem(coords[0, s], mine)


def first_kernel(
    coords, live, tiles, sketch, outer, own, partner, code, tbuf, panel, phl, acc, sems, panel_sem, *, rows
):
    cap = tiles.shape[0]
    k = sketch.shape[0]
    panel_copy = pltpu.make_async_copy(sketch, panel, panel_sem)
    panel_copy.start()
    start_tiles(live[0], tiles, tbuf, sems)
    acc[...] = jnp.zeros_like(acc)
    for s in range(cap):
        code[s] = slot_code(s, coords, live[0], outer.shape[0], phl.shape[0], rows)
    panel_copy.wait()
    keep_panel(lambda t: panel[:, t * T : (t + 1) * T], k, phl)
    each_chunk(
        live[0],
        cap,
        lambda s: spread_slot(code[s], *halves(tbuf[s]), phl, acc),
        lambda c: tile_copy(c, tiles, tbuf, sems).wait(),
    )
    put_spread(acc, (outer, own, partner))


def keep_spread(parts, shl):
    k = parts[0].shape[1]
    each = parts[0].shape[0]
    for n, part in enumerate(parts):

        def one(i, carry, part=part, n=n):
            hi, lo = halves(part[i])
            shl[n * each + i, :k, :] = hi
            shl[n * each + i, k:, :] = lo
            return carry

        lax.fori_loop(0, each, one, 0, unroll=4)
    shl[3 * each] = jnp.zeros_like(shl[3 * each])


def image_slot(entry, hi, lo, shl, img):
    k = shl.shape[1] // 2
    q = dot(shl[entry & 255], jnp.concatenate([hi, lo], axis=0), (1, 1))
    img[entry >> 8] += fold(q, k)


def whole_image(img):
    return jnp.concatenate([img[t] for t in range(img.shape[0])], axis=1)


def put_gram(image, out):
    g = dot(image, image, (1, 1), HIGHEST)
    h = g.shape[0] // 2
    quarters = (g[:h, :h], g[:h, h:], g[h:, h:])
    packed = jnp.concatenate(
        [jnp.concatenate([q[8 * r : 8 * r + 8] for r in range(h // 8)], axis=1) for q in quarters], axis=0
    )
    for n in range(out.shape[0]):
        out[n] = packed


def middle_kernel(
    code, live, tiles, s_outer, s_own, s_partner, outer, own, partner, gram,
    tbuf, thl, shl, img, phl, acc, sems,
):
    cap = tiles.shape[0]
    k = s_own.shape[1]
    start_tiles(live[0], tiles, tbuf, sems)
    keep_spread((s_outer, s_own, s_partner), shl)
    img[...] = jnp.zeros_like(img)
    acc[...] = jnp.zeros_like(acc)

    def forth(s):
        hi, lo = halves(tbuf[s])
        thl[s, :T, :] = hi
        thl[s, T:, :] = lo
        image_slot(code[s], hi, lo, shl, img)

    each_chunk(live[0], cap, forth, lambda c: tile_copy(c, tiles, tbuf, sems).wait())
    put_gram(whole_image(img), gram)
    keep_panel(lambda t: img[t], k, phl)
    each_chunk(live[0], cap, lambda s: spread_slot(code[s], thl[s, :T, :], thl[s, T:, :], phl, acc))
    put_spread(acc, (outer, own, partner))


def share_kernel(pieces, whole, gram):
    rows = whole.shape[1]
    total = pieces[0]
    for n in range(1, pieces.shape[0]):
        total = total + pieces[n]
    for n in range(whole.shape[0]):
        whole[n] = total[:rows]
    gram[...] = total[rows:]


def inverse_factor(g):
    k = g.shape[0]
    row_id = lax.broadcasted_iota(jnp.int32, (8, 2 * k), 0)
    eye = (lax.broadcasted_iota(jnp.int32, (k, k), 0) == lax.broadcasted_iota(jnp.int32, (k, k), 1)).astype(F32)
    full = jnp.concatenate([g, eye], axis=1)
    m = [full[8 * j : 8 * j + 8] for j in range(k // 8)]

    def row_of(x, r):
        return jnp.broadcast_to(x[r : r + 1, :], x.shape)

    for j in range(k // 8):
        rows = [row_of(m[j], t) for t in range(8)]
        cols = [
            {i: jnp.broadcast_to(m[i][:, 8 * j + t : 8 * j + t + 1], (8, 2 * k)) for i in range(j, k // 8)}
            for t in range(8)
        ]
        scale = jnp.zeros((8, 2 * k), F32)
        for t in range(8):
            pivot = row_of(cols[t][j], t)
            scale = jnp.where(row_id == t, lax.rsqrt(pivot), scale)
            inv = 1.0 / pivot
            q = rows[t] * inv
            cols[t][j] = jnp.where(row_id > t, cols[t][j], 0.0)
            for u in range(t + 1, 8):
                part = row_of(cols[t][j], u)
                f = part * inv
                rows[u] = rows[u] - part * q
                for i in range(j, k // 8):
                    cols[u][i] = cols[u][i] - cols[t][i] * f
            for i in range(j, k // 8):
                m[i] = m[i] - cols[t][i] * q
        m[j] = m[j] * scale
    return jnp.concatenate([x[:, k:] for x in m], axis=0)


def summed_gram(parts, k):
    packed = parts[0]
    for n in range(1, parts.shape[0]):
        packed = packed + parts[n]
    h = k // 2
    ul, ur, lr = (
        jnp.concatenate([packed[8 * q : 8 * q + 8, h * r : h * r + h] for r in range(h // 8)], axis=0) for q in range(3)
    )
    return jnp.concatenate([jnp.concatenate([ul, ur], axis=1), jnp.concatenate([ur.T, lr], axis=1)], axis=0)


def factor_kernel(parts, linv):
    linv[...] = inverse_factor(summed_gram(parts, linv.shape[0]))


def last_kernel(code, live, tiles, s_outer, s_own, s_partner, linv, image, gram, tbuf, shl, img, sems):
    start_tiles(live[0], tiles, tbuf, sems)
    keep_spread((s_outer, s_own, s_partner), shl)
    img[...] = jnp.zeros_like(img)
    each_chunk(
        live[0],
        tiles.shape[0],
        lambda s: image_slot(code[s], *halves(tbuf[s]), shl, img),
        lambda c: tile_copy(c, tiles, tbuf, sems).wait(),
    )
    x = dot(linv[...], whole_image(img), (1, 0), HIGHEST)
    image[...] = x
    put_gram(x, gram)


def basis_kernel(parts, image, basis, *, scale):
    linv = inverse_factor(summed_gram(parts, image.shape[0]))
    basis[...] = dot(linv, image[...], (1, 0), HIGHEST) * scale


def swapped(copies, axes):
    return lax.all_to_all(copies, axes, split_axis=0, concat_axis=0, tiled=True)


in_space = pltpu.with_memory_space_constraint


def to_everyone(x, axes):
    return swapped(jnp.broadcast_to(x, (lax.axis_size(axes), *x.shape)), axes)


VMEM = pl.BlockSpec(memory_space=pltpu.VMEM)
SMEM = pl.BlockSpec(memory_space=pltpu.SMEM)
HBM = pl.BlockSpec(memory_space=pltpu.HBM)


def call(kernel, ins, outs, scratch=(), prefetch=0, out_specs=None, limit=VMEM_LIMIT):
    return pl.pallas_call(
        kernel,
        grid_spec=pltpu.PrefetchScalarGridSpec(
            num_scalar_prefetch=prefetch,
            grid=(),
            in_specs=ins,
            out_specs=out_specs or [VMEM] * len(outs),
            scratch_shapes=scratch,
        ),
        out_shape=[jax.ShapeDtypeStruct(shape, dtype) for shape, dtype in outs],
        compiler_params=pltpu.CompilerParams(vmem_limit_bytes=limit),
    )


def local(tiles, coords, live, sketch):
    rows = lax.axis_size(ROWS)
    groups = lax.axis_size("grp")
    cap = tiles.shape[0]
    k = sketch.shape[1]
    mine = sketch.shape[0] // T
    block = groups * mine
    packed = (3 * 8, T)

    outer = [(r, (r - 1) % rows if r % 2 == 0 else (r + 1) % rows) for r in range(rows)]
    partner = [(r, r ^ 1) for r in range(rows)]

    tbuf = pltpu.VMEM((cap, T, T), F32)
    thl = pltpu.VMEM((cap, 2 * T, T), BF16)
    panel = pltpu.VMEM((k, mine * T), F32)
    phl = pltpu.VMEM((mine, 2 * k, T), BF16)
    shl = pltpu.VMEM((3 * block + 1, 2 * k, T), BF16)
    acc = pltpu.VMEM((3 * block + 1, k, T), F32)
    img = pltpu.VMEM((mine, k, T), F32)
    sems = pltpu.SemaphoreType.DMA((cap // CHUNK,))
    block_out = ((block, k, T), F32)

    def over_pairs(to_outer, to_partner):
        got_outer = lax.ppermute(to_outer, ROWS, outer)
        got_partner = lax.ppermute(to_partner, ROWS, partner)
        return got_outer, got_partner

    def pieces(x):
        return x.reshape(groups, mine * k, T)

    def exchange(parts):
        p_outer, p_own, p_partner = parts
        got_outer, got = over_pairs(p_outer, p_partner)
        total = p_own + got_outer + got
        own = to_everyone(swapped(pieces(total), "grp").sum(axis=0), "grp").reshape(block, k, T)
        at_outer, at_partner = over_pairs(own, own)
        return at_outer, own, at_partner

    def exchange_with_gram(parts, gram):
        p_outer, p_own, p_partner = parts
        gram = swapped(gram, "y")
        got_outer, got = over_pairs(p_outer, p_partner)
        total = pieces(p_own + got_outer + got)
        sides = jnp.broadcast_to(gram.sum(axis=0), (groups, *packed))
        arrived = swapped(jnp.concatenate([total, sides], axis=1), "grp")
        copies, gram = call(share_kernel, [VMEM], [((groups, mine * k, T), F32), (packed, F32)])(arrived)
        own = swapped(copies, "grp").reshape(block, k, T)
        beside = lax.ppermute(gram, ROWS, partner)
        copies = jnp.broadcast_to(gram + beside, (lax.axis_size("z"), *packed))
        own, copies = lax.optimization_barrier((own, copies))
        gram = swapped(copies, "z")
        at_outer, at_partner = over_pairs(own, own)
        return (at_outer, own, at_partner), gram

    *parts, code = call(
        functools.partial(first_kernel, rows=rows),
        [HBM, HBM],
        [block_out] * 3 + [((cap,), jnp.int32)],
        [tbuf, panel, phl, acc, sems, pltpu.SemaphoreType.DMA],
        2,
        [VMEM] * 3 + [SMEM],
    )(in_space(coords.T, pltpu.HBM), live, tiles, in_space(sketch.T, pltpu.HBM))
    whole = exchange(parts)
    *parts, gram = call(
        middle_kernel,
        [HBM] + [VMEM] * 3,
        [block_out] * 3 + [((lax.axis_size("y"), *packed), F32)],
        [tbuf, thl, shl, img, phl, acc, sems],
        2,
    )(code, live, tiles, *whole)
    whole, gram = exchange_with_gram(parts, gram)
    linv = call(factor_kernel, [VMEM], [((k, k), F32)])(gram)[0]
    image, gram = call(
        last_kernel, [HBM] + [VMEM] * 4, [((k, mine * T), F32), ((2 * groups, *packed), F32)], [tbuf, shl, img, sems], 2
    )(code, live, tiles, *whole, linv)
    gram = to_everyone(swapped(gram, ("c", "grp")).sum(axis=0), "z").sum(axis=0)
    scale = float(rows * groups * sketch.shape[0]) ** 0.5
    return call(
        functools.partial(basis_kernel, scale=scale), [VMEM] * 2, [(sketch.shape[::-1], F32)]
    )(to_everyone(gram, "y"), image)[0].T


def solution(mesh):
    finer = Mesh(mesh.devices.reshape(8, 8, 2, mesh.shape["grp"]), ROWS_GRP)
    placed = (P(ROWS_GRP, None, None), P(ROWS_GRP, None), P(ROWS_GRP), P(ROWS_GRP, None))
    return jax.shard_map(local, mesh=finer, in_specs=placed, out_specs=P(ROWS_GRP, None), check_vma=False)
```

```python
import functools

import jax
import jax.numpy as jnp
from jax import lax
from jax.experimental import pallas as pl
from jax.experimental.pallas import tpu as pltpu
from jax.sharding import Mesh
from jax.sharding import PartitionSpec as P


ROWS = ("y", "z", "c")
ROWS_GRP = ("y", "z", "c", "grp")
HIGHEST = lax.Precision.HIGHEST
F32 = jnp.float32
BF16 = jnp.bfloat16
T = 128
CHUNK = 8
L1, L2, L3 = 16 << 20, 16 << 20, 50 << 20
VMEM_LIMIT = 50 * 1024 * 1024
SMALL_LIMIT = 8 * 1024 * 1024


def dot(a, b, contract, precision=None):
    return lax.dot_general(
        a, b, ((contract[:1], contract[1:]), ((), ())), precision=precision, preferred_element_type=F32
    )


def halves(x):
    hi = x.astype(BF16)
    return hi, (x - hi.astype(F32)).astype(BF16)


def fold(q, k):
    return (q[:k, :T] + q[k:, T:]) + (q[k:, :T] + q[:k, T:])


def tile_copy(c, tiles, tbuf, sems):
    at = pl.ds(c * CHUNK, CHUNK)
    return pltpu.make_async_copy(tiles.at[at], tbuf.at[at], sems.at[c])


def start_tiles(live, tiles, tbuf, sems):
    for c in range(tiles.shape[0] // CHUNK):

        @pl.when(c * CHUNK < live)
        def _():
            tile_copy(c, tiles, tbuf, sems).start()


def each_chunk(live, cap, work, ready=None):
    for c in range(cap // CHUNK):

        @pl.when(c * CHUNK < live)
        def _():
            if ready is not None:
                ready(c)
            for s in range(c * CHUNK, (c + 1) * CHUNK):
                work(s)


def keep_panel(panel, k, phl):
    for t in range(phl.shape[0]):
        hi, lo = halves(panel(t))
        phl[t, :k, :] = hi
        phl[t, k:, :] = lo


def spread_slot(entry, hi, lo, phl, acc):
    k = phl.shape[1] // 2
    at = entry & 255
    q = dot(phl[entry >> 8], jnp.concatenate([hi, lo], axis=1), (1, 0))
    acc[at] += fold(q, k)


def put_spread(acc, outs):
    each = outs[0].shape[0]
    for n, out in enumerate(outs):
        out[...] = acc[n * each : (n + 1) * each]


def slot_code(s, coords, live, block, mine, rows):
    odd = lax.axis_index("c")
    row = (lax.axis_index("y") * lax.axis_size("z") + lax.axis_index("z")) * 2 + odd
    column = coords[1, s]
    step = lax.rem(lax.div(column, block) - row + 1 + rows, rows)
    step = jnp.where(odd == 1, 2 - step, step)
    place = jnp.where(s < live, step * block + lax.rem(column, block), 3 * block)
    return place + 256 * lax.rem(coords[0, s], mine)


def first_kernel(
    coords, live, tiles, sketch, outer, own, partner, code, thl, tbuf, panel, phl, acc, sems, panel_sem, *, rows
):
    cap = tiles.shape[0]
    k = sketch.shape[0]
    panel_copy = pltpu.make_async_copy(sketch, panel, panel_sem)
    panel_copy.start()
    start_tiles(live[0], tiles, tbuf, sems)
    acc[...] = jnp.zeros_like(acc)
    for s in range(cap):
        code[s] = slot_code(s, coords, live[0], outer.shape[0], phl.shape[0], rows)
    panel_copy.wait()
    keep_panel(lambda t: panel[:, t * T : (t + 1) * T], k, phl)

    def work(s):
        hi, lo = halves(tbuf[s])
        thl[s, :T, :] = hi
        thl[s, T:, :] = lo
        spread_slot(code[s], hi, lo, phl, acc)

    each_chunk(live[0], cap, work, lambda c: tile_copy(c, tiles, tbuf, sems).wait())
    put_spread(acc, (outer, own, partner))


def keep_spread(parts, shl):
    k = parts[0].shape[1]
    each = parts[0].shape[0]
    for n, part in enumerate(parts):

        def one(i, carry, part=part, n=n):
            hi, lo = halves(part[i])
            shl[n * each + i, :k, :] = hi
            shl[n * each + i, k:, :] = lo
            return carry

        lax.fori_loop(0, each, one, 0, unroll=4)
    shl[3 * each] = jnp.zeros_like(shl[3 * each])


def image_slot(entry, hl, shl, img):
    k = shl.shape[1] // 2
    img[entry >> 8] += fold(dot(shl[entry & 255], hl, (1, 1)), k)


def whole_image(img):
    return jnp.concatenate([img[t] for t in range(img.shape[0])], axis=1)


def put_gram(image, out):
    g = dot(image, image, (1, 1), HIGHEST)
    h = g.shape[0] // 2
    quarters = (g[:h, :h], g[:h, h:], g[h:, h:])
    packed = jnp.concatenate(
        [jnp.concatenate([q[8 * r : 8 * r + 8] for r in range(h // 8)], axis=1) for q in quarters], axis=0
    )
    for n in range(out.shape[0]):
        out[n] = packed


def middle_kernel(
    code, live, thl, s_outer, s_own, s_partner, outer, own, partner, gram, shl, img, phl, acc
):
    cap = thl.shape[0]
    k = s_own.shape[1]
    keep_spread((s_outer, s_own, s_partner), shl)
    img[...] = jnp.zeros_like(img)
    acc[...] = jnp.zeros_like(acc)
    each_chunk(live[0], cap, lambda s: image_slot(code[s], thl[s], shl, img))
    put_gram(whole_image(img), gram)
    keep_panel(lambda t: img[t], k, phl)
    each_chunk(live[0], cap, lambda s: spread_slot(code[s], thl[s, :T, :], thl[s, T:, :], phl, acc))
    put_spread(acc, (outer, own, partner))


def join_kernel(own, outer, partner, out):
    groups = out.shape[0]
    mine = own.shape[0] // groups
    k = own.shape[1]
    for t in range(own.shape[0]):
        at = (t % mine) * k
        out[t // mine, at : at + k, :] = own[t] + outer[t] + partner[t]


def sum_of(parts):
    total = parts[0]
    for n in range(1, parts.shape[0]):
        total = total + parts[n]
    return total


def fan_kernel(parts, copies):
    total = sum_of(parts)
    for n in range(copies.shape[0]):
        copies[n] = total


def share_kernel(pieces, whole, gram):
    rows = whole.shape[1]
    total = pieces[0]
    for n in range(1, pieces.shape[0]):
        total = total + pieces[n]
    for n in range(whole.shape[0]):
        whole[n] = total[:rows]
    gram[...] = total[rows:]


def inverse_factor(g):
    k = g.shape[0]
    row_id = lax.broadcasted_iota(jnp.int32, (8, 2 * k), 0)
    eye = (lax.broadcasted_iota(jnp.int32, (k, k), 0) == lax.broadcasted_iota(jnp.int32, (k, k), 1)).astype(F32)
    full = jnp.concatenate([g, eye], axis=1)
    m = [full[8 * j : 8 * j + 8] for j in range(k // 8)]

    def row_of(x, r):
        return jnp.broadcast_to(x[r : r + 1, :], x.shape)

    for j in range(k // 8):
        rows = [row_of(m[j], t) for t in range(8)]
        cols = [
            {i: jnp.broadcast_to(m[i][:, 8 * j + t : 8 * j + t + 1], (8, 2 * k)) for i in range(j, k // 8)}
            for t in range(8)
        ]
        scale = jnp.zeros((8, 2 * k), F32)
        for t in range(8):
            pivot = row_of(cols[t][j], t)
            scale = jnp.where(row_id == t, lax.rsqrt(pivot), scale)
            inv = 1.0 / pivot
            q = rows[t] * inv
            cols[t][j] = jnp.where(row_id > t, cols[t][j], 0.0)
            for u in range(t + 1, 8):
                part = row_of(cols[t][j], u)
                f = part * inv
                rows[u] = rows[u] - part * q
                for i in range(j, k // 8):
                    cols[u][i] = cols[u][i] - cols[t][i] * f
            for i in range(j, k // 8):
                m[i] = m[i] - cols[t][i] * q
        m[j] = m[j] * scale
    return jnp.concatenate([x[:, k:] for x in m], axis=0)


def summed_gram(parts, k):
    packed = parts[0]
    for n in range(1, parts.shape[0]):
        packed = packed + parts[n]
    h = k // 2
    ul, ur, lr = (
        jnp.concatenate([packed[8 * q : 8 * q + 8, h * r : h * r + h] for r in range(h // 8)], axis=0) for q in range(3)
    )
    return jnp.concatenate([jnp.concatenate([ul, ur], axis=1), jnp.concatenate([ur.T, lr], axis=1)], axis=0)


def factor_kernel(parts, linv):
    linv[...] = inverse_factor(summed_gram(parts, linv.shape[0]))


def last_kernel(code, live, tiles, s_outer, s_own, s_partner, linv, image, gram, tbuf, shl, img, sems):
    start_tiles(live[0], tiles, tbuf, sems)
    keep_spread((s_outer, s_own, s_partner), shl)
    img[...] = jnp.zeros_like(img)
    each_chunk(
        live[0],
        tiles.shape[0],
        lambda s: image_slot(code[s], jnp.concatenate(halves(tbuf[s]), axis=0), shl, img),
        lambda c: tile_copy(c, tiles, tbuf, sems).wait(),
    )
    x = dot(linv[...], whole_image(img), (1, 0), HIGHEST)
    image[...] = x
    put_gram(x, gram)


def basis_kernel(parts, image, basis, *, scale):
    linv = inverse_factor(summed_gram(parts, image.shape[0]))
    basis[...] = dot(linv, image[...], (1, 0), HIGHEST) * scale


def swapped(copies, axes):
    return lax.all_to_all(copies, axes, split_axis=0, concat_axis=0, tiled=True)


in_space = pltpu.with_memory_space_constraint


def to_everyone(x, axes):
    return swapped(jnp.broadcast_to(x, (lax.axis_size(axes), *x.shape)), axes)


VMEM = pl.BlockSpec(memory_space=pltpu.VMEM)
SMEM = pl.BlockSpec(memory_space=pltpu.SMEM)
HBM = pl.BlockSpec(memory_space=pltpu.HBM)


def call(kernel, ins, outs, scratch=(), prefetch=0, out_specs=None, limit=VMEM_LIMIT):
    return pl.pallas_call(
        kernel,
        grid_spec=pltpu.PrefetchScalarGridSpec(
            num_scalar_prefetch=prefetch,
            grid=(),
            in_specs=ins,
            out_specs=out_specs or [VMEM] * len(outs),
            scratch_shapes=scratch,
        ),
        out_shape=[jax.ShapeDtypeStruct(shape, dtype) for shape, dtype in outs],
        compiler_params=pltpu.CompilerParams(vmem_limit_bytes=limit),
    )


def local(tiles, coords, live, sketch):
    rows = lax.axis_size(ROWS)
    groups = lax.axis_size("grp")
    cap = tiles.shape[0]
    k = sketch.shape[1]
    mine = sketch.shape[0] // T
    block = groups * mine
    packed = (3 * 8, T)

    outer = [(r, (r - 1) % rows if r % 2 == 0 else (r + 1) % rows) for r in range(rows)]
    partner = [(r, r ^ 1) for r in range(rows)]

    tbuf = pltpu.VMEM((cap, T, T), F32)
    panel = pltpu.VMEM((k, mine * T), F32)
    phl = pltpu.VMEM((mine, 2 * k, T), BF16)
    shl = pltpu.VMEM((3 * block + 1, 2 * k, T), BF16)
    acc = pltpu.VMEM((3 * block + 1, k, T), F32)
    img = pltpu.VMEM((mine, k, T), F32)
    sems = pltpu.SemaphoreType.DMA((cap // CHUNK,))
    block_out = ((block, k, T), F32)

    def over_pairs(to_outer, to_partner):
        got_outer = lax.ppermute(to_outer, ROWS, outer)
        got_partner = lax.ppermute(to_partner, ROWS, partner)
        return got_outer, got_partner

    def small(kernel, outs, *args):
        return call(kernel, [VMEM] * len(args), outs, limit=SMALL_LIMIT)(*args)

    whole_out = ((groups, mine * k, T), F32)

    def exchange(parts):
        p_outer, p_own, p_partner = parts
        got_outer, got = over_pairs(p_outer, p_partner)
        (total,) = small(join_kernel, [whole_out], p_own, got_outer, got)
        (copies,) = small(fan_kernel, [whole_out], swapped(total, "grp"))
        own = swapped(copies, "grp").reshape(block, k, T)
        at_outer, at_partner = over_pairs(own, own)
        return at_outer, own, at_partner

    def exchange_with_gram(parts, gram):
        p_outer, p_own, p_partner = parts
        gram = swapped(gram, "y")
        got_outer, got = over_pairs(p_outer, p_partner)
        total = (p_own + got_outer + got).reshape(groups, mine * k, T)
        sides = jnp.broadcast_to(gram.sum(axis=0), (groups, *packed))
        arrived = swapped(jnp.concatenate([total, sides], axis=1), "grp")
        copies, gram = call(share_kernel, [VMEM], [((groups, mine * k, T), F32), (packed, F32)])(arrived)
        own = swapped(copies, "grp").reshape(block, k, T)
        beside = lax.ppermute(gram, ROWS, partner)
        own, gram = lax.optimization_barrier((own, gram + beside))
        gram = to_everyone(gram, "z")
        at_outer, at_partner = over_pairs(own, own)
        return (at_outer, own, at_partner), gram

    *parts, code, thl = call(
        functools.partial(first_kernel, rows=rows),
        [HBM, HBM],
        [block_out] * 3 + [((cap,), jnp.int32), ((cap, 2 * T, T), BF16)],
        [tbuf, panel, phl, acc, sems, pltpu.SemaphoreType.DMA],
        2,
        [VMEM] * 3 + [SMEM, VMEM],
        L1,
    )(in_space(coords.T, pltpu.HBM), live, in_space(tiles, pltpu.HBM), in_space(sketch.T, pltpu.HBM))
    whole = exchange(parts)
    *parts, gram = call(
        middle_kernel,
        [VMEM] * 4,
        [block_out] * 3 + [((lax.axis_size("y"), *packed), F32)],
        [shl, img, phl, acc],
        2,
        limit=L2,
    )(code, live, thl, *whole)
    whole, gram = exchange_with_gram(parts, gram)
    linv = call(factor_kernel, [VMEM], [((k, k), F32)], limit=SMALL_LIMIT)(gram)[0]
    image, gram = call(
        last_kernel,
        [HBM] + [VMEM] * 4,
        [((k, mine * T), F32), ((2 * groups, *packed), F32)],
        [tbuf, shl, img, sems],
        2,
        limit=L3,
    )(code, live, tiles, *whole, linv)
    gram = to_everyone(swapped(gram, ("c", "grp")).sum(axis=0), "z").sum(axis=0)
    scale = float(rows * groups * sketch.shape[0]) ** 0.5
    return call(
        functools.partial(basis_kernel, scale=scale), [VMEM] * 2, [(sketch.shape[::-1], F32)], limit=SMALL_LIMIT
    )(to_everyone(gram, "y"), image)[0].T


def solution(mesh):
    finer = Mesh(mesh.devices.reshape(8, 8, 2, mesh.shape["grp"]), ROWS_GRP)
    placed = (P(ROWS_GRP, None, None), P(ROWS_GRP, None), P(ROWS_GRP), P(ROWS_GRP, None))
    return jax.shard_map(local, mesh=finer, in_specs=placed, out_specs=P(ROWS_GRP, None), check_vma=False)
```

```python
import functools

import jax
import jax.numpy as jnp
from jax import lax
from jax.experimental import pallas as pl
from jax.experimental.pallas import tpu as pltpu
from jax.sharding import Mesh
from jax.sharding import PartitionSpec as P


ROWS = ("y", "z", "c")
ROWS_GRP = ("y", "z", "c", "grp")
HIGHEST = lax.Precision.HIGHEST
F32 = jnp.float32
BF16 = jnp.bfloat16
T = 128
CHUNK = 8
L1, L2, L3 = 16 << 20, 16 << 20, 50 << 20
VMEM_LIMIT = 50 * 1024 * 1024
SMALL_LIMIT = 8 * 1024 * 1024


def dot(a, b, contract, precision=None):
    return lax.dot_general(
        a, b, ((contract[:1], contract[1:]), ((), ())), precision=precision, preferred_element_type=F32
    )


def halves(x):
    hi = x.astype(BF16)
    return hi, (x - hi.astype(F32)).astype(BF16)


def fold(q, k):
    return (q[:k, :T] + q[k:, T:]) + (q[k:, :T] + q[:k, T:])


def tile_copy(c, tiles, tbuf, sems):
    at = pl.ds(c * CHUNK, CHUNK)
    return pltpu.make_async_copy(tiles.at[at], tbuf.at[at], sems.at[c])


def start_tiles(live, tiles, tbuf, sems):
    for c in range(tiles.shape[0] // CHUNK):

        @pl.when(c * CHUNK < live)
        def _():
            tile_copy(c, tiles, tbuf, sems).start()


def each_chunk(live, cap, work, ready=None):
    for c in range(cap // CHUNK):

        @pl.when(c * CHUNK < live)
        def _():
            if ready is not None:
                ready(c)
            for s in range(c * CHUNK, (c + 1) * CHUNK):
                work(s)


def keep_panel(panel, k, phl):
    for t in range(phl.shape[0]):
        hi, lo = halves(panel(t))
        phl[t, :k, :] = hi
        phl[t, k:, :] = lo


def spread_slot(entry, hi, lo, phl, acc):
    k = phl.shape[1] // 2
    at = entry & 255
    q = dot(phl[entry >> 8], jnp.concatenate([hi, lo], axis=1), (1, 0))
    acc[at] += fold(q, k)


def put_spread(acc, outs):
    each = outs[0].shape[0]
    for n, out in enumerate(outs):
        out[...] = acc[n * each : (n + 1) * each]


def slot_code(s, coords, live, block, mine, rows):
    odd = lax.axis_index("c")
    row = (lax.axis_index("y") * lax.axis_size("z") + lax.axis_index("z")) * 2 + odd
    column = coords[1, s]
    step = lax.rem(lax.div(column, block) - row + 1 + rows, rows)
    step = jnp.where(odd == 1, 2 - step, step)
    place = jnp.where(s < live, step * block + lax.rem(column, block), 3 * block)
    return place + 256 * lax.rem(coords[0, s], mine)


def first_kernel(
    live, coords_in, tiles, sketch, outer, own, partner, code, thl,
    coords, tbuf, panel, phl, acc, sems, panel_sem, coords_sem, *, rows
):
    cap = tiles.shape[0]
    k = sketch.shape[0]
    panel_copy = pltpu.make_async_copy(sketch, panel, panel_sem)
    panel_copy.start()
    coords_copy = pltpu.make_async_copy(coords_in, coords, coords_sem)
    coords_copy.start()
    start_tiles(live[0], tiles, tbuf, sems)
    acc[...] = jnp.zeros_like(acc)
    coords_copy.wait()
    for s in range(cap):
        code[s] = slot_code(s, coords, live[0], outer.shape[0], phl.shape[0], rows)
    panel_copy.wait()
    keep_panel(lambda t: panel[:, t * T : (t + 1) * T], k, phl)

    def work(s):
        hi, lo = halves(tbuf[s])
        thl[s, :T, :] = hi
        thl[s, T:, :] = lo
        spread_slot(code[s], hi, lo, phl, acc)

    each_chunk(live[0], cap, work, lambda c: tile_copy(c, tiles, tbuf, sems).wait())
    put_spread(acc, (outer, own, partner))


def keep_spread(parts, shl):
    k = parts[0].shape[1]
    each = parts[0].shape[0]
    for n, part in enumerate(parts):

        def one(i, carry, part=part, n=n):
            hi, lo = halves(part[i])
            shl[n * each + i, :k, :] = hi
            shl[n * each + i, k:, :] = lo
            return carry

        lax.fori_loop(0, each, one, 0, unroll=4)
    shl[3 * each] = jnp.zeros_like(shl[3 * each])


def image_slot(entry, hl, shl, img):
    k = shl.shape[1] // 2
    img[entry >> 8] += fold(dot(shl[entry & 255], hl, (1, 1)), k)


def whole_image(img):
    return jnp.concatenate([img[t] for t in range(img.shape[0])], axis=1)


def put_gram(image, out):
    g = dot(image, image, (1, 1), HIGHEST)
    h = g.shape[0] // 2
    quarters = (g[:h, :h], g[:h, h:], g[h:, h:])
    packed = jnp.concatenate(
        [jnp.concatenate([q[8 * r : 8 * r + 8] for r in range(h // 8)], axis=1) for q in quarters], axis=0
    )
    for n in range(out.shape[0]):
        out[n] = packed


def middle_kernel(
    code, live, thl, s_outer, s_own, s_partner, outer, own, partner, gram, shl, img, phl, acc
):
    cap = thl.shape[0]
    k = s_own.shape[1]
    keep_spread((s_outer, s_own, s_partner), shl)
    img[...] = jnp.zeros_like(img)
    acc[...] = jnp.zeros_like(acc)
    each_chunk(live[0], cap, lambda s: image_slot(code[s], thl[s], shl, img))
    put_gram(whole_image(img), gram)
    keep_panel(lambda t: img[t], k, phl)
    each_chunk(live[0], cap, lambda s: spread_slot(code[s], thl[s, :T, :], thl[s, T:, :], phl, acc))
    put_spread(acc, (outer, own, partner))


def join_kernel(own, outer, partner, out):
    groups = out.shape[0]
    mine = own.shape[0] // groups
    k = own.shape[1]
    for t in range(own.shape[0]):
        at = (t % mine) * k
        out[t // mine, at : at + k, :] = own[t] + outer[t] + partner[t]


def sum_of(parts):
    total = parts[0]
    for n in range(1, parts.shape[0]):
        total = total + parts[n]
    return total


def fan_kernel(parts, copies):
    total = sum_of(parts)
    for n in range(copies.shape[0]):
        copies[n] = total


def pair_kernel(one, other, copies):
    total = one[...] + other[...]
    for n in range(copies.shape[0]):
        copies[n] = total


def share_kernel(pieces, whole, gram):
    rows = whole.shape[1]
    total = pieces[0]
    for n in range(1, pieces.shape[0]):
        total = total + pieces[n]
    for n in range(whole.shape[0]):
        whole[n] = total[:rows]
    gram[...] = total[rows:]


def inverse_factor(g):
    k = g.shape[0]
    row_id = lax.broadcasted_iota(jnp.int32, (8, 2 * k), 0)
    eye = (lax.broadcasted_iota(jnp.int32, (k, k), 0) == lax.broadcasted_iota(jnp.int32, (k, k), 1)).astype(F32)
    full = jnp.concatenate([g, eye], axis=1)
    m = [full[8 * j : 8 * j + 8] for j in range(k // 8)]

    def row_of(x, r):
        return jnp.broadcast_to(x[r : r + 1, :], x.shape)

    for j in range(k // 8):
        rows = [row_of(m[j], t) for t in range(8)]
        cols = [
            {i: jnp.broadcast_to(m[i][:, 8 * j + t : 8 * j + t + 1], (8, 2 * k)) for i in range(j, k // 8)}
            for t in range(8)
        ]
        scale = jnp.zeros((8, 2 * k), F32)
        for t in range(8):
            pivot = row_of(cols[t][j], t)
            scale = jnp.where(row_id == t, lax.rsqrt(pivot), scale)
            inv = 1.0 / pivot
            q = rows[t] * inv
            cols[t][j] = jnp.where(row_id > t, cols[t][j], 0.0)
            for u in range(t + 1, 8):
                part = row_of(cols[t][j], u)
                f = part * inv
                rows[u] = rows[u] - part * q
                for i in range(j, k // 8):
                    cols[u][i] = cols[u][i] - cols[t][i] * f
            for i in range(j, k // 8):
                m[i] = m[i] - cols[t][i] * q
        m[j] = m[j] * scale
    return jnp.concatenate([x[:, k:] for x in m], axis=0)


def summed_gram(parts, k):
    packed = parts[0]
    for n in range(1, parts.shape[0]):
        packed = packed + parts[n]
    h = k // 2
    ul, ur, lr = (
        jnp.concatenate([packed[8 * q : 8 * q + 8, h * r : h * r + h] for r in range(h // 8)], axis=0) for q in range(3)
    )
    return jnp.concatenate([jnp.concatenate([ul, ur], axis=1), jnp.concatenate([ur.T, lr], axis=1)], axis=0)


def factor_kernel(parts, linv):
    linv[...] = inverse_factor(summed_gram(parts, linv.shape[0]))


def last_kernel(code, live, tiles, s_outer, s_own, s_partner, linv, image, gram, tbuf, shl, img, sems):
    start_tiles(live[0], tiles, tbuf, sems)
    keep_spread((s_outer, s_own, s_partner), shl)
    img[...] = jnp.zeros_like(img)
    each_chunk(
        live[0],
        tiles.shape[0],
        lambda s: image_slot(code[s], jnp.concatenate(halves(tbuf[s]), axis=0), shl, img),
        lambda c: tile_copy(c, tiles, tbuf, sems).wait(),
    )
    x = dot(linv[...], whole_image(img), (1, 0), HIGHEST)
    image[...] = x
    put_gram(x, gram)


def basis_kernel(parts, image, basis, *, scale):
    linv = inverse_factor(summed_gram(parts, image.shape[0]))
    basis[...] = dot(linv, image[...], (1, 0), HIGHEST) * scale


def swapped(copies, axes):
    return lax.all_to_all(copies, axes, split_axis=0, concat_axis=0, tiled=True)


in_space = pltpu.with_memory_space_constraint


def to_everyone(x, axes):
    return swapped(jnp.broadcast_to(x, (lax.axis_size(axes), *x.shape)), axes)


VMEM = pl.BlockSpec(memory_space=pltpu.VMEM)
SMEM = pl.BlockSpec(memory_space=pltpu.SMEM)
HBM = pl.BlockSpec(memory_space=pltpu.HBM)


def call(kernel, ins, outs, scratch=(), prefetch=0, out_specs=None, limit=VMEM_LIMIT):
    return pl.pallas_call(
        kernel,
        grid_spec=pltpu.PrefetchScalarGridSpec(
            num_scalar_prefetch=prefetch,
            grid=(),
            in_specs=ins,
            out_specs=out_specs or [VMEM] * len(outs),
            scratch_shapes=scratch,
        ),
        out_shape=[jax.ShapeDtypeStruct(shape, dtype) for shape, dtype in outs],
        compiler_params=pltpu.CompilerParams(vmem_limit_bytes=limit),
    )


def local(tiles, coords, live, sketch):
    rows = lax.axis_size(ROWS)
    groups = lax.axis_size("grp")
    cap = tiles.shape[0]
    k = sketch.shape[1]
    mine = sketch.shape[0] // T
    block = groups * mine
    packed = (3 * 8, T)

    outer = [(r, (r - 1) % rows if r % 2 == 0 else (r + 1) % rows) for r in range(rows)]
    partner = [(r, r ^ 1) for r in range(rows)]

    tbuf = pltpu.VMEM((cap, T, T), F32)
    panel = pltpu.VMEM((k, mine * T), F32)
    phl = pltpu.VMEM((mine, 2 * k, T), BF16)
    shl = pltpu.VMEM((3 * block + 1, 2 * k, T), BF16)
    acc = pltpu.VMEM((3 * block + 1, k, T), F32)
    img = pltpu.VMEM((mine, k, T), F32)
    sems = pltpu.SemaphoreType.DMA((cap // CHUNK,))
    block_out = ((block, k, T), F32)

    def over_pairs(to_outer, to_partner):
        got_outer = lax.ppermute(to_outer, ROWS, outer)
        got_partner = lax.ppermute(to_partner, ROWS, partner)
        return got_outer, got_partner

    def small(kernel, outs, *args):
        return call(kernel, [VMEM] * len(args), outs, limit=SMALL_LIMIT)(*args)

    whole_out = ((groups, mine * k, T), F32)

    def exchange(parts):
        p_outer, p_own, p_partner = parts
        got_outer, got = over_pairs(p_outer, p_partner)
        (total,) = small(join_kernel, [whole_out], p_own, got_outer, got)
        (copies,) = small(fan_kernel, [whole_out], swapped(total, "grp"))
        own = swapped(copies, "grp").reshape(block, k, T)
        at_outer, at_partner = over_pairs(own, own)
        return at_outer, own, at_partner

    def exchange_with_gram(parts, gram):
        p_outer, p_own, p_partner = parts
        gram = swapped(gram, "y")
        got_outer, got = over_pairs(p_outer, p_partner)
        total = (p_own + got_outer + got).reshape(groups, mine * k, T)
        sides = jnp.broadcast_to(gram.sum(axis=0), (groups, *packed))
        arrived = swapped(jnp.concatenate([total, sides], axis=1), "grp")
        copies, gram = call(share_kernel, [VMEM], [((groups, mine * k, T), F32), (packed, F32)])(arrived)
        own = swapped(copies, "grp").reshape(block, k, T)
        beside = lax.ppermute(gram, ROWS, partner)
        (copies,) = small(pair_kernel, [((lax.axis_size("z"), *packed), F32)], gram, beside)
        own, copies = lax.optimization_barrier((own, copies))
        gram = swapped(copies, "z")
        at_outer, at_partner = over_pairs(own, own)
        return (at_outer, own, at_partner), gram

    *parts, code, thl = call(
        functools.partial(first_kernel, rows=rows),
        [HBM] * 3,
        [block_out] * 3 + [((cap,), jnp.int32), ((cap, 2 * T, T), BF16)],
        [pltpu.SMEM((2, cap), jnp.int32), tbuf, panel, phl, acc, sems, pltpu.SemaphoreType.DMA, pltpu.SemaphoreType.DMA],
        1,
        [VMEM] * 3 + [SMEM, VMEM],
        L1,
    )(live, in_space(coords.T, pltpu.HBM), in_space(tiles, pltpu.HBM), in_space(sketch.T, pltpu.HBM))
    whole = exchange(parts)
    *parts, gram = call(
        middle_kernel,
        [VMEM] * 4,
        [block_out] * 3 + [((lax.axis_size("y"), *packed), F32)],
        [shl, img, phl, acc],
        2,
        limit=L2,
    )(code, live, thl, *whole)
    whole, gram = exchange_with_gram(parts, gram)
    linv = call(factor_kernel, [VMEM], [((k, k), F32)], limit=SMALL_LIMIT)(gram)[0]
    image, gram = call(
        last_kernel,
        [HBM] + [VMEM] * 4,
        [((k, mine * T), F32), ((2 * groups, *packed), F32)],
        [tbuf, shl, img, sems],
        2,
        limit=L3,
    )(code, live, tiles, *whole, linv)
    gram = to_everyone(swapped(gram, ("c", "grp")).sum(axis=0), "z").sum(axis=0)
    scale = float(rows * groups * sketch.shape[0]) ** 0.5
    return call(
        functools.partial(basis_kernel, scale=scale), [VMEM] * 2, [(sketch.shape[::-1], F32)], limit=SMALL_LIMIT
    )(to_everyone(gram, "y"), image)[0].T


def solution(mesh):
    finer = Mesh(mesh.devices.reshape(8, 8, 2, mesh.shape["grp"]), ROWS_GRP)
    placed = (P(ROWS_GRP, None, None), P(ROWS_GRP, None), P(ROWS_GRP), P(ROWS_GRP, None))
    return jax.shard_map(local, mesh=finer, in_specs=placed, out_specs=P(ROWS_GRP, None), check_vma=False)
```

```python
import functools

import jax
import jax.numpy as jnp
from jax import lax
from jax.experimental import pallas as pl
from jax.experimental.pallas import tpu as pltpu
from jax.sharding import Mesh
from jax.sharding import PartitionSpec as P


ROWS = ("y", "z", "c")
ROWS_GRP = ("y", "z", "c", "grp")
HIGHEST = lax.Precision.HIGHEST
F32 = jnp.float32
BF16 = jnp.bfloat16
T = 128
CHUNK = 8
KEPT = 8
L1, L2, L3 = 16 << 20, 16 << 20, 50 << 20
VMEM_LIMIT = 50 * 1024 * 1024
SMALL_LIMIT = 8 * 1024 * 1024


def dot(a, b, contract, precision=None):
    return lax.dot_general(
        a, b, ((contract[:1], contract[1:]), ((), ())), precision=precision, preferred_element_type=F32
    )


def halves(x):
    hi = x.astype(BF16)
    return hi, (x - hi.astype(F32)).astype(BF16)


def fold(q, k):
    return (q[:k, :T] + q[k:, T:]) + (q[k:, :T] + q[:k, T:])


def tile_copy(c, tiles, tbuf, sems):
    at = pl.ds(c * CHUNK, CHUNK)
    return pltpu.make_async_copy(tiles.at[at], tbuf.at[at], sems.at[c])


def start_tiles(live, tiles, tbuf, sems, skip=0):
    for c in range(skip // CHUNK, tiles.shape[0] // CHUNK):

        @pl.when(c * CHUNK < live)
        def _():
            tile_copy(c, tiles, tbuf, sems).start()


def each_chunk(live, cap, work, ready=None):
    for c in range(cap // CHUNK):

        @pl.when(c * CHUNK < live)
        def _():
            if ready is not None:
                ready(c)
            for s in range(c * CHUNK, (c + 1) * CHUNK):
                work(s)


def keep_panel(panel, k, phl):
    for t in range(phl.shape[0]):
        hi, lo = halves(panel(t))
        phl[t, :k, :] = hi
        phl[t, k:, :] = lo


def spread_slot(entry, hi, lo, phl, acc):
    k = phl.shape[1] // 2
    at = entry & 255
    q = dot(phl[entry >> 8], jnp.concatenate([hi, lo], axis=1), (1, 0))
    acc[at] += fold(q, k)


def put_spread(acc, outs):
    each = outs[0].shape[0]
    for n, out in enumerate(outs):
        out[...] = acc[n * each : (n + 1) * each]


def slot_code(s, coords, live, block, mine, rows):
    odd = lax.axis_index("c")
    row = (lax.axis_index("y") * lax.axis_size("z") + lax.axis_index("z")) * 2 + odd
    column = coords[1, s]
    step = lax.rem(lax.div(column, block) - row + 1 + rows, rows)
    step = jnp.where(odd == 1, 2 - step, step)
    place = jnp.where(s < live, step * block + lax.rem(column, block), 3 * block)
    return place + 256 * lax.rem(coords[0, s], mine)


def first_kernel(
    live, coords_in, tiles, sketch, outer, own, partner, code, kept, thl,
    coords, tbuf, panel, phl, acc, sems, panel_sem, coords_sem, *, rows
):
    cap = tiles.shape[0]
    k = sketch.shape[0]
    panel_copy = pltpu.make_async_copy(sketch, panel, panel_sem)
    panel_copy.start()
    coords_copy = pltpu.make_async_copy(coords_in, coords, coords_sem)
    coords_copy.start()
    start_tiles(live[0], tiles, tbuf, sems)
    acc[...] = jnp.zeros_like(acc)
    coords_copy.wait()
    for s in range(cap):
        code[s] = slot_code(s, coords, live[0], outer.shape[0], phl.shape[0], rows)
    panel_copy.wait()
    keep_panel(lambda t: panel[:, t * T : (t + 1) * T], k, phl)

    def work(s):
        hi, lo = halves(tbuf[s])
        here, at = (kept, s) if s < KEPT else (thl, s - KEPT)
        here[at, :T, :] = hi
        here[at, T:, :] = lo
        spread_slot(code[s], hi, lo, phl, acc)

    each_chunk(live[0], cap, work, lambda c: tile_copy(c, tiles, tbuf, sems).wait())
    put_spread(acc, (outer, own, partner))


def keep_spread(parts, shl):
    k = parts[0].shape[1]
    each = parts[0].shape[0]
    for n, part in enumerate(parts):

        def one(i, carry, part=part, n=n):
            hi, lo = halves(part[i])
            shl[n * each + i, :k, :] = hi
            shl[n * each + i, k:, :] = lo
            return carry

        lax.fori_loop(0, each, one, 0, unroll=4)
    shl[3 * each] = jnp.zeros_like(shl[3 * each])


def image_slot(entry, hl, shl, img):
    k = shl.shape[1] // 2
    img[entry >> 8] += fold(dot(shl[entry & 255], hl, (1, 1)), k)


def whole_image(img):
    return jnp.concatenate([img[t] for t in range(img.shape[0])], axis=1)


def put_gram(image, out):
    g = dot(image, image, (1, 1), HIGHEST)
    h = g.shape[0] // 2
    quarters = (g[:h, :h], g[:h, h:], g[h:, h:])
    packed = jnp.concatenate(
        [jnp.concatenate([q[8 * r : 8 * r + 8] for r in range(h // 8)], axis=1) for q in quarters], axis=0
    )
    for n in range(out.shape[0]):
        out[n] = packed


def middle_kernel(
    code, live, kept, thl, s_outer, s_own, s_partner, outer, own, partner, gram, shl, img, phl, acc
):
    cap = kept.shape[0] + thl.shape[0]
    k = s_own.shape[1]

    def split(s):
        return kept[s] if s < KEPT else thl[s - KEPT]

    def back(s):
        hl = split(s)
        spread_slot(code[s], hl[:T], hl[T:], phl, acc)

    keep_spread((s_outer, s_own, s_partner), shl)
    img[...] = jnp.zeros_like(img)
    acc[...] = jnp.zeros_like(acc)
    each_chunk(live[0], cap, lambda s: image_slot(code[s], split(s), shl, img))
    put_gram(whole_image(img), gram)
    keep_panel(lambda t: img[t], k, phl)
    each_chunk(live[0], cap, back)
    put_spread(acc, (outer, own, partner))


def join_kernel(own, outer, partner, out):
    groups = out.shape[0]
    mine = own.shape[0] // groups
    k = own.shape[1]
    for t in range(own.shape[0]):
        at = (t % mine) * k
        out[t // mine, at : at + k, :] = own[t] + outer[t] + partner[t]


def sum_of(parts):
    total = parts[0]
    for n in range(1, parts.shape[0]):
        total = total + parts[n]
    return total


def fan_kernel(parts, copies):
    total = sum_of(parts)
    for n in range(copies.shape[0]):
        copies[n] = total


def pair_kernel(one, other, copies):
    total = one[...] + other[...]
    for n in range(copies.shape[0]):
        copies[n] = total


def share_kernel(pieces, whole, gram):
    rows = whole.shape[1]
    total = pieces[0]
    for n in range(1, pieces.shape[0]):
        total = total + pieces[n]
    for n in range(whole.shape[0]):
        whole[n] = total[:rows]
    gram[...] = total[rows:]


def inverse_factor(g):
    k = g.shape[0]
    row_id = lax.broadcasted_iota(jnp.int32, (8, 2 * k), 0)
    eye = (lax.broadcasted_iota(jnp.int32, (k, k), 0) == lax.broadcasted_iota(jnp.int32, (k, k), 1)).astype(F32)
    full = jnp.concatenate([g, eye], axis=1)
    m = [full[8 * j : 8 * j + 8] for j in range(k // 8)]

    def row_of(x, r):
        return jnp.broadcast_to(x[r : r + 1, :], x.shape)

    for j in range(k // 8):
        rows = [row_of(m[j], t) for t in range(8)]
        cols = [
            {i: jnp.broadcast_to(m[i][:, 8 * j + t : 8 * j + t + 1], (8, 2 * k)) for i in range(j, k // 8)}
            for t in range(8)
        ]
        scale = jnp.zeros((8, 2 * k), F32)
        for t in range(8):
            pivot = row_of(cols[t][j], t)
            scale = jnp.where(row_id == t, lax.rsqrt(pivot), scale)
            inv = 1.0 / pivot
            q = rows[t] * inv
            cols[t][j] = jnp.where(row_id > t, cols[t][j], 0.0)
            for u in range(t + 1, 8):
                part = row_of(cols[t][j], u)
                f = part * inv
                rows[u] = rows[u] - part * q
                for i in range(j, k // 8):
                    cols[u][i] = cols[u][i] - cols[t][i] * f
            for i in range(j, k // 8):
                m[i] = m[i] - cols[t][i] * q
        m[j] = m[j] * scale
    return jnp.concatenate([x[:, k:] for x in m], axis=0)


def summed_gram(parts, k):
    packed = parts[0]
    for n in range(1, parts.shape[0]):
        packed = packed + parts[n]
    h = k // 2
    ul, ur, lr = (
        jnp.concatenate([packed[8 * q : 8 * q + 8, h * r : h * r + h] for r in range(h // 8)], axis=0) for q in range(3)
    )
    return jnp.concatenate([jnp.concatenate([ul, ur], axis=1), jnp.concatenate([ur.T, lr], axis=1)], axis=0)


def factor_kernel(parts, linv):
    linv[...] = inverse_factor(summed_gram(parts, linv.shape[0]))


def last_kernel(code, live, tiles, kept, s_outer, s_own, s_partner, linv, image, gram, tbuf, shl, img, sems):
    start_tiles(live[0], tiles, tbuf, sems, KEPT)
    keep_spread((s_outer, s_own, s_partner), shl)
    img[...] = jnp.zeros_like(img)

    def ready(c):
        if c * CHUNK >= KEPT:
            tile_copy(c, tiles, tbuf, sems).wait()

    def work(s):
        hl = kept[s] if s < KEPT else jnp.concatenate(halves(tbuf[s]), axis=0)
        image_slot(code[s], hl, shl, img)

    each_chunk(live[0], tiles.shape[0], work, ready)
    x = dot(linv[...], whole_image(img), (1, 0), HIGHEST)
    image[...] = x
    put_gram(x, gram)


def basis_kernel(parts, image, basis, *, scale):
    linv = inverse_factor(summed_gram(parts, image.shape[0]))
    basis[...] = dot(linv, image[...], (1, 0), HIGHEST) * scale


def swapped(copies, axes):
    return lax.all_to_all(copies, axes, split_axis=0, concat_axis=0, tiled=True)


in_space = pltpu.with_memory_space_constraint


def to_everyone(x, axes):
    return swapped(jnp.broadcast_to(x, (lax.axis_size(axes), *x.shape)), axes)


VMEM = pl.BlockSpec(memory_space=pltpu.VMEM)
SMEM = pl.BlockSpec(memory_space=pltpu.SMEM)
HBM = pl.BlockSpec(memory_space=pltpu.HBM)


def call(kernel, ins, outs, scratch=(), prefetch=0, out_specs=None, limit=VMEM_LIMIT):
    return pl.pallas_call(
        kernel,
        grid_spec=pltpu.PrefetchScalarGridSpec(
            num_scalar_prefetch=prefetch,
            grid=(),
            in_specs=ins,
            out_specs=out_specs or [VMEM] * len(outs),
            scratch_shapes=scratch,
        ),
        out_shape=[jax.ShapeDtypeStruct(shape, dtype) for shape, dtype in outs],
        compiler_params=pltpu.CompilerParams(vmem_limit_bytes=limit),
    )


def local(tiles, coords, live, sketch):
    rows = lax.axis_size(ROWS)
    groups = lax.axis_size("grp")
    cap = tiles.shape[0]
    k = sketch.shape[1]
    mine = sketch.shape[0] // T
    block = groups * mine
    packed = (3 * 8, T)

    outer = [(r, (r - 1) % rows if r % 2 == 0 else (r + 1) % rows) for r in range(rows)]
    partner = [(r, r ^ 1) for r in range(rows)]

    tbuf = pltpu.VMEM((cap, T, T), F32)
    panel = pltpu.VMEM((k, mine * T), F32)
    phl = pltpu.VMEM((mine, 2 * k, T), BF16)
    shl = pltpu.VMEM((3 * block + 1, 2 * k, T), BF16)
    acc = pltpu.VMEM((3 * block + 1, k, T), F32)
    img = pltpu.VMEM((mine, k, T), F32)
    sems = pltpu.SemaphoreType.DMA((cap // CHUNK,))
    block_out = ((block, k, T), F32)

    def over_pairs(to_outer, to_partner):
        got_outer = lax.ppermute(to_outer, ROWS, outer)
        got_partner = lax.ppermute(to_partner, ROWS, partner)
        return got_outer, got_partner

    def small(kernel, outs, *args):
        return call(kernel, [VMEM] * len(args), outs, limit=SMALL_LIMIT)(*args)

    whole_out = ((groups, mine * k, T), F32)

    def exchange(parts):
        p_outer, p_own, p_partner = parts
        got_outer, got = over_pairs(p_outer, p_partner)
        (total,) = small(join_kernel, [whole_out], p_own, got_outer, got)
        (copies,) = small(fan_kernel, [whole_out], swapped(total, "grp"))
        own = swapped(copies, "grp").reshape(block, k, T)
        at_outer, at_partner = over_pairs(own, own)
        return at_outer, own, at_partner

    def exchange_with_gram(parts, gram):
        p_outer, p_own, p_partner = parts
        gram = swapped(gram, "y")
        got_outer, got = over_pairs(p_outer, p_partner)
        total = (p_own + got_outer + got).reshape(groups, mine * k, T)
        sides = jnp.broadcast_to(gram.sum(axis=0), (groups, *packed))
        arrived = swapped(jnp.concatenate([total, sides], axis=1), "grp")
        copies, gram = call(share_kernel, [VMEM], [((groups, mine * k, T), F32), (packed, F32)])(arrived)
        own = swapped(copies, "grp").reshape(block, k, T)
        beside = lax.ppermute(gram, ROWS, partner)
        (copies,) = small(pair_kernel, [((lax.axis_size("z"), *packed), F32)], gram, beside)
        own, copies = lax.optimization_barrier((own, copies))
        gram = swapped(copies, "z")
        at_outer, at_partner = over_pairs(own, own)
        return (at_outer, own, at_partner), gram

    *parts, code, kept, thl = call(
        functools.partial(first_kernel, rows=rows),
        [HBM] * 3,
        [block_out] * 3 + [((cap,), jnp.int32), ((KEPT, 2 * T, T), BF16), ((cap - KEPT, 2 * T, T), BF16)],
        [pltpu.SMEM((2, cap), jnp.int32), tbuf, panel, phl, acc, sems, pltpu.SemaphoreType.DMA, pltpu.SemaphoreType.DMA],
        1,
        [VMEM] * 3 + [SMEM, VMEM, VMEM],
        L1,
    )(live, in_space(coords.T, pltpu.HBM), in_space(tiles, pltpu.HBM), in_space(sketch.T, pltpu.HBM))
    whole = exchange(parts)
    *parts, gram = call(
        middle_kernel,
        [VMEM] * 5,
        [block_out] * 3 + [((lax.axis_size("y"), *packed), F32)],
        [shl, img, phl, acc],
        2,
        limit=L2,
    )(code, live, kept, thl, *whole)
    whole, gram = exchange_with_gram(parts, gram)
    linv = call(factor_kernel, [VMEM], [((k, k), F32)], limit=SMALL_LIMIT)(gram)[0]
    image, gram = call(
        last_kernel,
        [HBM] + [VMEM] * 5,
        [((k, mine * T), F32), ((2 * groups, *packed), F32)],
        [tbuf, shl, img, sems],
        2,
        limit=L3,
    )(code, live, tiles, kept, *whole, linv)
    gram = to_everyone(swapped(gram, ("c", "grp")).sum(axis=0), "z").sum(axis=0)
    scale = float(rows * groups * sketch.shape[0]) ** 0.5
    return call(
        functools.partial(basis_kernel, scale=scale), [VMEM] * 2, [(sketch.shape[::-1], F32)], limit=SMALL_LIMIT
    )(to_everyone(gram, "y"), image)[0].T


def solution(mesh):
    finer = Mesh(mesh.devices.reshape(8, 8, 2, mesh.shape["grp"]), ROWS_GRP)
    placed = (P(ROWS_GRP, None, None), P(ROWS_GRP, None), P(ROWS_GRP), P(ROWS_GRP, None))
    return jax.shard_map(local, mesh=finer, in_specs=placed, out_specs=P(ROWS_GRP, None), check_vma=False)
```
